128 devices in a mesh: store: 64 (over x, y, z), rep: 2 (over core).
Axes of the slice: x: 4, y: 4, z: 4, core: 2. Of those that a mesh axis runs over, the one named last changes fastest.
Arguments:
- features: bfloat16 [131072, 768], P('store'), may hold values from -6 to 6
- owners_near: int32 [65536, 1], P(('store', 'rep')), may hold values from 0 to 63; in each aligned block of 512 rows (0 to 511, 512 to 1023, ...) at most 16 rows name the same one
- slots_near: int32 [65536, 1], P(('store', 'rep')), may hold values from 0 to 2047
- owners_far: int32 [393216, 1], P(('store', 'rep')), may hold values from 0 to 63; in each aligned block of 3072 rows (0 to 3071, 3072 to 6143, ...) at most 96 rows name the same one
- slots_far: int32 [393216, 1], P(('store', 'rep')), may hold values from 0 to 2047
- adjacency_low: int32 [65536, 15], P(('store', 'rep')), may hold values from 0 to 3583
- adjacency_top: int32 [16384, 10], P(('store', 'rep')), may hold values from 0 to 511
- labels: int32 [16384], P(('store', 'rep')), may hold values from 0 to 152
- weights_low: float32 [1536, 1024], replicated, may hold values from -0.15625 to 0.15625
- weights_top: float32 [2048, 153], replicated, may hold values from -0.25 to 0.25
- first_low: float32 [1536, 1024], P(('store', 'rep')), may hold values from -0.00390625 to 0.00390625
- second_low: float32 [1536, 1024], P(('store', 'rep')), may hold values from 1e-09 to 1e-07
- first_top: float32 [2048, 153], P(('store', 'rep')), may hold values from -0.03125 to 0.03125
- second_top: float32 [2048, 153], P(('store', 'rep')), may hold values from 1e-07 to 1e-05
Outputs:
- logits: float32 [16384, 153], P(('store', 'rep'))
- new_low: float32 [1536, 1024], replicated
- new_first_low: float32 [1536, 1024], P(('store', 'rep'))
- new_second_low: float32 [1536, 1024], P(('store', 'rep'))
- new_top: float32 [2048, 153], replicated
- new_first_top: float32 [2048, 153], P(('store', 'rep'))
- new_second_top: float32 [2048, 153], P(('store', 'rep'))
The draws below stay inside these ranges and needn't reach their ends.
Inputs may be any that keep to these rules, and one draw needn't show every extreme that they name: `owners_near`: within the rows of one trainer, no store index is named more than 16 times, and some index is named exactly that often. `owners_far`: within the rows of one trainer, no store index is named more than 96 times, and some index is named exactly that often.
All inputs are finite; a program needn't handle non-finite values.
Results may differ from the reference program's by a relative error of at most 0.005.
Values may be sent and summed in bfloat16 or wider, within the bound.
A program may use at most 128 MiB of HBM per device.

```python
import math
import jax
import jax.numpy as jnp
import numpy as np
from jax import lax

FEAT = 768
HIDDEN_SIZE = 1024
CLASSES = 153
SEEDS = 128
NEAR = 512
FAR = 3072
NODES_DEV = 2048
FAN_TOP = 10
FAN_LOW = 15
TRAINERS = 128
NODES = 131072
CAP_NEAR = 16
CAP_FAR = 96
N_STORE = 64


def plant(array, stream_key, least, top_value):
    shape = array.shape
    index_at = [jax.random.randint(jax.random.fold_in(stream_key, axis), (), 0, shape[axis]) for axis in range(len(shape))]
    array = array.at[tuple(index_at)].set(least)
    longest = shape.index(max(shape))
    index_at[longest] = (index_at[longest] + 1) % shape[longest]
    return array.at[tuple(index_at)].set(top_value)


def levels(own_key, dims, shards, least, largest):
    level = 1.0
    for axis_at, blocks in shards:
        draws = jax.random.uniform(jax.random.fold_in(jax.random.fold_in(own_key, 6), axis_at), (blocks,), jnp.float32, least / len(shards), largest / len(shards))
        level = level * jnp.repeat(jnp.exp(draws), dims[axis_at] // blocks).reshape((-1,) + (1,) * (len(dims) - 1 - axis_at))
    return level


def assign_block(rng, own, number, rows, count, top, most, skew):
    ranking = jax.random.permutation(rng, count)
    packed, ordinary = shares(count, rows * top, most, skew, True), shares(count, rows * top, most, skew, False)
    places = jnp.arange(count)

    def named(tallies, turn):
        used = int((tallies > 0).sum())
        fixed = max(1, used // 4)
        passed = fixed + (places - fixed + turn * (used - fixed)) % max(1, count - fixed)
        return jnp.zeros((count,), jnp.int32).at[ranking[jnp.where(places < fixed, places, passed)]].set(jnp.asarray(tallies, jnp.int32))

    tallies = jnp.where(number % 4 == 0, named(packed, number // 4), named(ordinary, number - number // 4 - 1))
    mixed = jax.random.permutation(jax.random.fold_in(own, 3), count)
    donor, taker = mixed[0:count // 2 * 2:2], mixed[1:count // 2 * 2:2]
    room = jnp.minimum(tallies[donor] - 1, most - tallies[taker]) // 2
    room = jnp.where((donor == ranking[0]) | (taker == ranking[0]) | (tallies[taker] == 0), 0, jnp.maximum(room, 0))
    passed = jax.random.randint(jax.random.fold_in(own, 4), (count // 2,), 0, 1 << 20) % (room + 1)
    tallies = tallies.at[donor].add(-passed).at[taker].add(passed)
    members = jnp.searchsorted(jnp.cumsum(tallies), jnp.arange(rows * top), side="right").astype(jnp.int32)
    listing = members.reshape(top, rows).T
    listing = listing[jax.random.permutation(jax.random.fold_in(own, 1), rows)]
    turn = jax.random.randint(jax.random.fold_in(own, 2), (rows, 1), 0, top)
    return jnp.take_along_axis(listing, (jnp.arange(top)[None, :] + turn) % top, axis=1)


def shares(count, total, bound, slope, full):
    weights = [(1 << 20) // math.isqrt(rank ** slope) + 1 for rank in range(1, count + 1)]
    largest = bound if full else min(bound, max(-(-total // count), total * weights[0] // sum(weights)))
    least = 1 if total - largest >= count - 1 else 0
    given, rest = [largest] + [least] * (count - 1), total - largest - least * (count - 1)
    while rest > 0:
        movable = [i for i in range(1, count) if given[i] < largest] or [i for i in range(1, count) if given[i] < bound]
        mass, budget = sum([weights[i] for i in movable]), rest
        for i in movable:
            extra = min(bound - given[i], max(1, budget * weights[i] // mass), rest)
            given[i] = given[i] + extra
            rest = rest - extra
    return np.array(given)


def bell_draw(rng, shape, deviation, limit, split=(), held_as=jnp.bfloat16):
    result = deviation * jax.random.normal(rng, shape, jnp.float32)
    if split:
        result = result * levels(rng, shape, split, -0.22, 0.18)
    return jnp.clip(result, -limit, limit).astype(held_as)


def setup_inputs(seed: int = 0) -> dict:
    key_of = jax.random.split(jax.random.key(seed), 15)
    features = bell_draw(key_of[0], (NODES, FEAT), 1.0, 6.0, ((0, 64),))
    owners_near_keys = jax.random.split(jax.random.fold_in(key_of[1], 1), (TRAINERS * NEAR) // NEAR)
    owners_near_turns = jax.random.permutation(jax.random.fold_in(key_of[1], 3), (TRAINERS * NEAR) // NEAR)
    owners_near = jax.vmap(lambda own, number: assign_block(jax.random.fold_in(key_of[1], 2), own, number, NEAR, N_STORE, 1, CAP_NEAR, 2))(owners_near_keys, owners_near_turns).reshape((TRAINERS * NEAR, 1))
    slots_near = plant(jax.random.randint(key_of[2], (TRAINERS * NEAR, 1), 0, NODES_DEV), jax.random.fold_in(key_of[2], 1), 0, NODES_DEV - 1).astype(jnp.int32)
    owners_far_keys = jax.random.split(jax.random.fold_in(key_of[3], 1), (TRAINERS * FAR) // FAR)
    owners_far_turns = jax.random.permutation(jax.random.fold_in(key_of[3], 3), (TRAINERS * FAR) // FAR)
    owners_far = jax.vmap(lambda own, number: assign_block(jax.random.fold_in(key_of[3], 2), own, number, FAR, N_STORE, 1, CAP_FAR, 2))(owners_far_keys, owners_far_turns).reshape((TRAINERS * FAR, 1))
    slots_far = plant(jax.random.randint(key_of[4], (TRAINERS * FAR, 1), 0, NODES_DEV), jax.random.fold_in(key_of[4], 1), 0, NODES_DEV - 1).astype(jnp.int32)
    adjacency_low = plant(jax.random.randint(key_of[5], (TRAINERS * NEAR, FAN_LOW), 0, NEAR + FAR), jax.random.fold_in(key_of[5], 1), 0, (NEAR + FAR) - 1).astype(jnp.int32)
    adjacency_top = plant(jax.random.randint(key_of[6], (TRAINERS * SEEDS, FAN_TOP), 0, NEAR), jax.random.fold_in(key_of[6], 1), 0, NEAR - 1).astype(jnp.int32)
    labels = plant(jax.random.randint(key_of[7], (TRAINERS * SEEDS,), 0, CLASSES), jax.random.fold_in(key_of[7], 1), 0, CLASSES - 1).astype(jnp.int32)
    weights_low = bell_draw(key_of[8], (2 * FEAT, HIDDEN_SIZE), (2 * FEAT) ** -0.5, 0.15625, (), jnp.float32)
    weights_top = bell_draw(key_of[9], (2 * HIDDEN_SIZE, CLASSES), (HIDDEN_SIZE // 2) ** -0.5, 0.25, (), jnp.float32)
    first_low = bell_draw(key_of[10], (2 * FEAT, HIDDEN_SIZE), 0.0003, 0.00390625, ((0, 128),), jnp.float32)
    second_low = jnp.clip(jnp.exp(math.log(1.0000000116860974e-07) - 4.6051702 * jax.random.uniform(key_of[11], (2 * FEAT, HIDDEN_SIZE), jnp.float32) ** levels(key_of[11], (2 * FEAT, HIDDEN_SIZE), ((0, 128),), -0.2, 0.2)), 9.999999717180685e-10, 1.0000000116860974e-07)
    first_top = bell_draw(key_of[12], (2 * HIDDEN_SIZE, CLASSES), 0.002, 0.03125, ((0, 128),), jnp.float32)
    second_top = jnp.clip(jnp.exp(math.log(9.999999747378752e-06) - 4.6051701 * jax.random.uniform(key_of[13], (2 * HIDDEN_SIZE, CLASSES), jnp.float32) ** levels(key_of[13], (2 * HIDDEN_SIZE, CLASSES), ((0, 128),), -0.2, 0.2)), 1.0000000116860974e-07, 9.999999747378752e-06)
    return {"features": features, "owners_near": owners_near, "slots_near": slots_near, "owners_far": owners_far, "slots_far": slots_far, "adjacency_low": adjacency_low, "adjacency_top": adjacency_top, "labels": labels, "weights_low": weights_low, "weights_top": weights_top, "first_low": first_low, "second_low": second_low, "first_top": first_top, "second_top": second_top}


beta_one = 0.9
beta_two = 0.999
bias_one = 1.0 - 0.9 ** 10
bias_two = 1.0 - 0.999 ** 10
learn_rate = 0.01
adam_eps = 1e-08

def gelu_tanh(values):
    return jax.nn.gelu(values, approximate=True)

def local_step(fetched, adjacency_low, adjacency_top, labels, low_bf, top_bf, scale):
    near_rows = adjacency_low.shape[0]
    seed_rows = labels.shape[0]
    width = top_bf.shape[0] // 2
    classes_all = top_bf.shape[1]
    gathered = jnp.zeros((near_rows, fetched.shape[1]), jnp.float32)
    for column in range(adjacency_low.shape[1]):
        gathered = gathered + fetched[adjacency_low[:, column]].astype(jnp.float32)
    low_mean = (gathered / adjacency_low.shape[1]).astype(jnp.bfloat16)
    low_input = jnp.concatenate([fetched[:near_rows], low_mean], axis=1)
    pre_hidden = jnp.dot(low_input, low_bf, preferred_element_type=jnp.float32)
    hidden = gelu_tanh(pre_hidden).astype(jnp.bfloat16)
    top_sum = jnp.zeros((seed_rows, width), jnp.float32)
    for column in range(adjacency_top.shape[1]):
        top_sum = top_sum + hidden[adjacency_top[:, column]].astype(jnp.float32)
    top_mean = (top_sum / adjacency_top.shape[1]).astype(jnp.bfloat16)
    top_input = jnp.concatenate([hidden[:seed_rows], top_mean], axis=1)
    logits = jnp.dot(top_input, top_bf, preferred_element_type=jnp.float32)
    powers = jnp.exp(logits)
    chances = powers / lax.optimization_barrier(jnp.sum(powers, axis=1, keepdims=True))
    targets = (labels[:, None] == jnp.arange(classes_all, dtype=jnp.int32)[None, :]).astype(jnp.float32)
    dlogits = ((chances - targets) * scale).astype(jnp.bfloat16)
    grad_top = lax.dot_general(top_input, dlogits, (((0,), (0,)), ((), ())), preferred_element_type=jnp.float32)
    dinput = lax.dot_general(dlogits, top_bf, (((1,), (1,)), ((), ())), preferred_element_type=jnp.float32)
    dhidden = jnp.zeros((near_rows, width), jnp.float32).at[:seed_rows].add(dinput[:, :width])
    spread = dinput[:, width:] / adjacency_top.shape[1]
    for column in range(adjacency_top.shape[1]):
        dhidden = dhidden.at[adjacency_top[:, column]].add(spread)
    unused, pullback = jax.vjp(gelu_tanh, pre_hidden)
    dpre = pullback(dhidden)[0].astype(jnp.bfloat16)
    grad_low = lax.dot_general(low_input, dpre, (((0,), (0,)), ((), ())), preferred_element_type=jnp.float32)
    return (logits, grad_low, grad_top)

def adam_update(weight, moment, square, gradient):
    moment_new = beta_one * moment + (1.0 - beta_one) * gradient
    square_new = beta_two * square + (1.0 - beta_two) * gradient * gradient
    update = moment_new / bias_one / (jnp.sqrt(square_new / bias_two) + adam_eps)
    return (weight - learn_rate * update, moment_new, square_new)

def reference(features, owners_near, slots_near, owners_far, slots_far, adjacency_low, adjacency_top, labels, weights_low, weights_top, first_low, second_low, first_top, second_top):
    trainers = owners_near.shape[0] // NEAR
    near_ids = (owners_near[:, 0] * NODES_DEV + slots_near[:, 0]).reshape(trainers, NEAR)
    far_ids = (owners_far[:, 0] * NODES_DEV + slots_far[:, 0]).reshape(trainers, -1)
    low_lists = adjacency_low.reshape(trainers, NEAR, -1)
    top_lists = adjacency_top.reshape(trainers, SEEDS, -1)
    label_rows = labels.reshape(trainers, SEEDS)
    low_bf = weights_low.astype(jnp.bfloat16)
    top_bf = weights_top.astype(jnp.bfloat16)
    scale = 1.0 / (trainers * SEEDS)

    def one_trainer(totals, pieces):
        near_part, far_part, low_part, top_part, label_part = pieces
        fetched = features[jnp.concatenate([near_part, far_part])]
        logit_rows, grad_low, grad_top = local_step(fetched, low_part, top_part, label_part, low_bf, top_bf, scale)
        return ((totals[0] + grad_low, totals[1] + grad_top), logit_rows)
    start = (jnp.zeros(weights_low.shape, jnp.float32), jnp.zeros(weights_top.shape, jnp.float32))
    (grad_low, grad_top), logit_all = lax.scan(one_trainer, start, (near_ids, far_ids, low_lists, top_lists, label_rows))
    new_low, new_first_low, new_second_low = adam_update(weights_low, first_low, second_low, grad_low)
    new_top, new_first_top, new_second_top = adam_update(weights_top, first_top, second_top, grad_top)
    return (logit_all.reshape(trainers * SEEDS, CLASSES), new_low, new_first_low, new_second_low, new_top, new_first_top, new_second_top)
```

```python
import functools

import jax
import jax.numpy as jnp
from jax import lax
from jax.experimental import pallas as pl
from jax.experimental.pallas import tpu as pltpu
from jax.sharding import PartitionSpec as P

beta_one = 0.9
beta_two = 0.999
bias_one = 1.0 - 0.9**10
bias_two = 1.0 - 0.999**10
learn_rate = 0.01
adam_eps = 1e-08

MESH = pl.DeviceIdType.MESH
F32 = jnp.float32
BF16 = jnp.bfloat16
SIDE = 4
STORES = SIDE**3
CAP_NEAR = 16
CAP_FAR = 96
CAP = CAP_NEAR + CAP_FAR
STRIDE, UNSTRIDE = 37, 45


def iota(shape, dim):
    return lax.broadcasted_iota(jnp.int32, shape, dim)


def dot(a, b):
    return jnp.dot(a, b, preferred_element_type=F32)


def dot_nt(a, b):
    return lax.dot_general(a, b, (((1,), (1,)), ((), ())), preferred_element_type=F32)


def place():
    store = lax.axis_index("store")
    rep = lax.axis_index("rep")
    return (store // 16, lax.rem(store // 4, 4), lax.rem(store, 4)), rep, 1 - 2 * rep


def partner(slot, chip, sign):
    shift = lax.rem(slot * STRIDE, STORES)
    steps = (shift // 16, lax.rem(shift // 4, 4), lax.rem(shift, 4))
    x, y, z = [lax.rem(at + sign * step + SIDE, SIDE) for at, step in zip(chip, steps)]
    return (x * SIDE + y) * SIDE + z


def fetch_kernel(
    own, slots, adj, feat, out,
    table, cols, req_out, req_in, counts, send, recv, total, marks,
    ask_send, ask_recv, row_send, row_recv,
):
    chip, rep, sign = place()
    barrier = pltpu.get_barrier_semaphore()

    @pl.loop(1, STORES)
    def _(i):
        pl.semaphore_signal(
            barrier, inc=1, device_id=(partner(i, chip, sign), rep), device_id_type=MESH
        )

    table[...] = jnp.zeros_like(table)
    upper = (iota((256, 256), 0) < iota((256, 256), 1)).astype(BF16)
    base = jnp.zeros((STORES, 1), F32)
    high = jnp.zeros((STORES, 128), F32)
    low = jnp.zeros((STORES, 128), F32)
    near_blocks = adj.shape[0] // 256
    for b in range(own.shape[1] // 256):
        span = slice(256 * b, 256 * b + 256)
        if b == near_blocks:
            base = jnp.zeros((STORES, 1), F32)
        owner = own[:, span]
        wanted = slots[:, span]
        jx = (sign * (chip[0] - (owner >> 4))) & 3
        jy = (sign * (chip[1] - ((owner >> 2) & 3))) & 3
        jz = (sign * (chip[2] - (owner & 3))) & 3
        slot = (((jx * 16) + jy * 4 + jz) * UNSTRIDE) & 63
        owned = (iota((STORES, 256), 0) == slot).astype(F32)
        owned_bf = owned.astype(BF16)
        before = dot(owned_bf, upper) + base
        base = base + jnp.sum(owned, axis=1, keepdims=True)
        position = jnp.sum(owned * before, axis=0, keepdims=True)
        if b >= near_blocks:
            position = position + CAP_NEAR
        slot_f = slot.astype(F32)
        for half in range(2):
            part = slice(128 * half, 128 * half + 128)
            table[2 * b + half : 2 * b + half + 1, 0:128] = slot_f[:, part]
            table[2 * b + half : 2 * b + half + 1, 128:256] = position[:, part]
        placed = (iota((128, 256), 0) == position.astype(jnp.int32)).astype(F32)
        high = high + dot_nt(owned_bf, (placed * (wanted >> 6).astype(F32)).astype(BF16))
        low = low + dot_nt(owned_bf, (placed * (wanted & 63).astype(F32)).astype(BF16))
    requests = (high * 64.0 + low).astype(jnp.int32)
    for i in range(STORES):
        req_out[i] = requests[i : i + 1, :]
    req_in[0] = requests[0:1, :]

    pl.semaphore_wait(barrier, STORES - 1)

    def ask(i):
        return pltpu.make_async_remote_copy(
            src_ref=req_out.at[i], dst_ref=req_in.at[i],
            send_sem=ask_send.at[i], recv_sem=ask_recv.at[i],
            device_id=(partner(i, chip, -sign), rep), device_id_type=MESH,
        )

    def give(i):
        return pltpu.make_async_remote_copy(
            src_ref=send.at[i], dst_ref=recv.at[i],
            send_sem=row_send.at[i], recv_sem=row_recv.at[i],
            device_id=(partner(i, chip, sign), rep), device_id_type=MESH,
        )

    @pl.loop(1, STORES)
    def _(i):
        ask(i).start()

    table_bf = table[...].astype(BF16)
    near_rows = adj.shape[0]
    for k in range(adj.shape[1]):
        entry = adj[:, k : k + 1]
        row_mark = (iota((near_rows, 32), 1) == (entry >> 7)).astype(F32).astype(BF16)
        found = dot(row_mark, table_bf)
        column = found[:, 0:128] * float(CAP) + found[:, 128:256]
        lane = iota((near_rows, 128), 1) == (entry & 127)
        cols[:, k : k + 1] = jnp.sum(jnp.where(lane, column, 0.0), axis=1, keepdims=True)

    @pl.loop(1, STORES)
    def _(i):
        ask(i).wait()

    asked = jnp.concatenate(
        [req_in[i].astype(F32) for i in range(STORES)] + [jnp.zeros((64, 128), F32)], axis=0
    )
    asked = jnp.transpose(asked)[0:CAP, :]
    total[0:CAP, 0:128] = asked

    nodes = feat.shape[0]

    @pl.loop(0, STORES // 4)
    def _(g):
        for m in range(4):
            i = g * 4 + m
            lane = iota((CAP, 128), 1) == i
            row = jnp.sum(jnp.where(lane, total[0:CAP, 0:128], 0.0), axis=1, keepdims=True)
            row = row.astype(jnp.int32)
            for c in range(nodes // 512):
                marks[CAP * m : CAP * m + CAP, 512 * c : 512 * c + 512] = (
                    (iota((CAP, 512), 1) + 512 * c == row).astype(F32).astype(BF16)
                )
        for h in range(3):
            span = slice(256 * h, 256 * h + 256)
            rows = dot(marks[...], feat[:, span]).astype(BF16)
            for m in range(4):
                send[g * 4 + m, :, span] = rows[CAP * m : CAP * m + CAP]
        for m in range(4):
            i = g * 4 + m

            @pl.when(i > 0)
            def _():
                give(i).start()

    recv[0] = send[0]

    groups, width = counts.shape[0], counts.shape[2]

    @pl.loop(0, near_rows // 32)
    def _(r):
        rows = pl.ds(pl.multiple_of(r * 32, 32), 32)
        mine = pl.ds(pl.multiple_of(near_rows + r * 32, 32), 32)
        picked = cols[rows, :]
        for c in range(groups):
            lane = (iota((32, width), 1) + width * c).astype(F32)
            tally = jnp.zeros((32, width), F32)
            for k in range(15):
                tally = tally + jnp.where(lane == picked[:, k : k + 1], 1.0, 0.0)
            counts[c, rows, :] = tally.astype(BF16)
            counts[c, mine, :] = jnp.where(lane == picked[:, 15:16], 1.0, 0.0).astype(BF16)

    total[...] = jnp.zeros_like(total)

    @pl.loop(0, groups)
    def _(c):
        for m in range(STORES // groups):
            i = c * (STORES // groups) + m

            @pl.when(i > 0)
            def _():
                give(i).wait_recv()

        block = recv[pl.ds(c * (STORES // groups), STORES // groups)].reshape(width, recv.shape[2])
        for h in range(3):
            span = slice(256 * h, 256 * h + 256)
            total[:, span] += dot(counts[c], block[:, span])

    features = recv.shape[2]
    out[:, 0:features] = total[near_rows : 2 * near_rows, :].astype(BF16)
    out[:, features : 2 * features] = (total[0:near_rows, :] / 15.0).astype(BF16)

    @pl.loop(1, STORES)
    def _(i):
        give(i).wait_send()


def fetch(owners, slots, adjacency, features):
    near = adjacency.shape[0]
    width = features.shape[1]
    groups = 8
    vmem = pl.BlockSpec(memory_space=pltpu.VMEM)
    return pl.pallas_call(
        fetch_kernel,
        out_shape=jax.ShapeDtypeStruct((near, 2 * width), BF16),
        in_specs=[vmem] * 4,
        out_specs=vmem,
        scratch_shapes=[
            pltpu.VMEM((32, 256), F32),
            pltpu.VMEM((near, 16), F32),
            pltpu.VMEM((STORES, 1, 128), jnp.int32),
            pltpu.VMEM((STORES, 1, 128), jnp.int32),
            pltpu.VMEM((groups, 2 * near, STORES // groups * CAP), BF16),
            pltpu.VMEM((STORES, CAP, width), BF16),
            pltpu.VMEM((STORES, CAP, width), BF16),
            pltpu.VMEM((2 * near, width), F32),
            pltpu.VMEM((4 * CAP, features.shape[0]), BF16),
            pltpu.SemaphoreType.DMA((STORES,)),
            pltpu.SemaphoreType.DMA((STORES,)),
            pltpu.SemaphoreType.DMA((STORES,)),
            pltpu.SemaphoreType.DMA((STORES,)),
        ],
        compiler_params=pltpu.CompilerParams(
            collective_id=0, has_side_effects=True, vmem_limit_bytes=58 << 20
        ),
    )(owners, slots, adjacency, features)


def spread_low():
    row, column = iota((384, 512), 0), iota((384, 512), 1)
    inner = column & 15
    return ((inner < 12) & (row == 12 * (column >> 4) + inner)).astype(F32).astype(BF16)


def spread_low_t():
    column, row = iota((512, 384), 1), iota((512, 384), 0)
    inner = row & 15
    return ((inner < 12) & (column == 12 * (row >> 4) + inner)).astype(F32).astype(BF16)


def spread_top(b):
    row, column = iota((256, 256), 0), iota((256, 256), 1)
    inner = column & 15
    return (
        ((inner >= 12) & (row == (column & -16) + 4 * (inner - 12) + b)).astype(F32).astype(BF16)
    )


def spread_top_t(b):
    column, row = iota((256, 256), 1), iota((256, 256), 0)
    inner = row & 15
    return (
        ((inner >= 12) & (column == (row & -16) + 4 * (inner - 12) + b)).astype(F32).astype(BF16)
    )


def gelu_parts(v):
    root = 0.7978845608028654
    square = v * v
    t = jnp.tanh(root * (v + 0.044715 * (v * square)))
    gate = 0.5 * (1.0 + t)
    slope = gate + 0.5 * v * (1.0 - t * t) * (root * (1.0 + 3.0 * 0.044715 * square))
    return v * gate, slope


def step_kernel(scale, x, wl, wt, at, at_t, lab, logits_out, grads, wtb, hidden, slope, dpre, left):
    classes = wt.shape[1]
    width = wl.shape[1]
    seeds = at.shape[0]
    near = x.shape[0]
    wtb[...] = jnp.zeros_like(wtb)
    wtb[:, 0:classes] = wt[...].astype(BF16)
    for n in range(width // 256):
        span = slice(256 * n, 256 * n + 256)
        value, rise = gelu_parts(dot(x[...], wl[:, span].astype(BF16)))
        hidden[:, span] = value.astype(BF16)
        slope[:, span] = rise
    fan = at.shape[1]
    picks = jnp.zeros((seeds, near), F32)
    picks_t = jnp.zeros((near, seeds), F32)
    for k in range(fan):
        picks = picks + (iota((seeds, near), 1) == at[:, k : k + 1]).astype(F32)
        picks_t = picks_t + (iota((near, seeds), 0) == at_t[k : k + 1, :]).astype(F32)
    picks = picks.astype(BF16)
    picks_t = picks_t.astype(BF16)
    mean = (dot(picks, hidden[...]) / float(fan)).astype(BF16)
    own = hidden[0:seeds, :]
    logits = dot(own, wtb[0:width, :]) + dot(mean, wtb[width : 2 * width, :])
    logits_out[...] = logits[:, 0:classes]
    lane = iota(logits.shape, 1)
    powers = jnp.where(lane < classes, jnp.exp(logits), 0.0)
    chances = powers / jnp.sum(powers, axis=1, keepdims=True)
    targets = (lane == lab[...]).astype(F32)
    dlogits = ((chances - targets) * scale).astype(BF16)
    first = dot_nt(dlogits, wtb[0:width, :])
    second = dot_nt(dlogits, wtb[width : 2 * width, :]) / float(fan)
    second_high = second.astype(BF16)
    second_low = (second - second_high.astype(F32)).astype(BF16)
    for n in range(width // 256):
        span = slice(256 * n, 256 * n + 256)
        back = dot(picks_t, second_high[:, span]) + dot(picks_t, second_low[:, span])
        dpre[seeds:near, span] = (back[seeds:near] * slope[seeds:near, span]).astype(BF16)
        dpre[0:seeds, span] = ((back[0:seeds] + first[:, span]) * slope[0:seeds, span]).astype(BF16)
    low_t = spread_low_t()
    for m in range(x.shape[1] // 384):
        left[512 * m : 512 * m + 512, :] = dot_nt(low_t, x[:, 384 * m : 384 * m + 384]).astype(BF16)
    for b in range(width // 256):
        span = slice(256 * b, 256 * b + 256)
        top_t = spread_top_t(b)
        for m in range(2 * width // 256):
            source = own if m < width // 256 else mean
            at_col = 256 * (m % (width // 256))
            top_left = dot_nt(top_t, source[:, at_col : at_col + 256]).astype(BF16)
            rows = slice(256 * m, 256 * m + 256)
            grads[rows, span] = (dot(left[rows, :], dpre[:, span]) + dot(top_left, dlogits)).astype(BF16)


def local_step(x, weights_low, weights_top, adjacency_top, labels, scale):
    near = x.shape[0]
    seeds, fan = adjacency_top.shape
    width = weights_low.shape[1]
    vmem = pl.BlockSpec(memory_space=pltpu.VMEM)
    return pl.pallas_call(
        functools.partial(step_kernel, scale),
        out_shape=(
            jax.ShapeDtypeStruct((seeds, weights_top.shape[1]), F32),
            jax.ShapeDtypeStruct((2 * width, width), BF16),
        ),
        in_specs=[vmem] * 6,
        out_specs=(vmem, vmem),
        scratch_shapes=[
            pltpu.VMEM((2 * width, 256), BF16),
            pltpu.VMEM((near, width), BF16),
            pltpu.VMEM((near, width), F32),
            pltpu.VMEM((near, width), BF16),
            pltpu.VMEM((2 * width, near), BF16),
        ],
        compiler_params=pltpu.CompilerParams(vmem_limit_bytes=48 << 20),
    )(x, weights_low, weights_top, adjacency_top, adjacency_top.T, labels[:, None])


def adam_parts(moment, square, gradient):
    moment_new = beta_one * moment + (1.0 - beta_one) * gradient
    square_new = beta_two * square + (1.0 - beta_two) * gradient * gradient
    update = moment_new / bias_one / (jnp.sqrt(square_new / bias_two) + adam_eps)
    return learn_rate * update, moment_new, square_new


def reduce_kernel(
    grads, ml, vl, mt, vt, everyone, ml_out, vl_out, mt_out, vt_out,
    pair, halves, parts, share, top, pair_send, pair_recv, part_send, part_recv,
    all_send, all_recv, twin_send, twin_recv,
):
    chip, rep, sign = place()
    me = lax.axis_index("store")
    other = 1 - rep
    classes = mt.shape[1]
    barrier = pltpu.get_barrier_semaphore()

    @pl.loop(1, STORES)
    def _(i):
        pl.semaphore_signal(
            barrier, inc=1, device_id=(partner(i, chip, sign), rep), device_id_type=MESH
        )

    pl.semaphore_signal(barrier, inc=1, device_id=(me, other), device_id_type=MESH)
    pl.semaphore_wait(barrier, STORES)

    swap = pltpu.make_async_remote_copy(
        src_ref=grads.at[:, other], dst_ref=pair, send_sem=pair_send, recv_sem=pair_recv,
        device_id=(me, other), device_id_type=MESH,
    )
    swap.start()
    swap.wait()

    def hand(i):
        return pltpu.make_async_remote_copy(
            src_ref=halves.at[i], dst_ref=parts.at[i],
            send_sem=part_send.at[i], recv_sem=part_recv.at[i],
            device_id=(partner(i, chip, sign), rep), device_id_type=MESH,
        )

    @pl.loop(0, STORES)
    def _(i):
        to = partner(i, chip, sign)
        halves[i] = (grads[to, rep].astype(F32) + pair[to].astype(F32)).astype(BF16)

        @pl.when(i > 0)
        def _():
            hand(i).start()

    def add(i, so_far):
        hand(i).wait_recv()
        return so_far + parts[i].astype(F32)

    gradient = lax.fori_loop(1, STORES, add, halves[0].astype(F32))

    step, moment, square = adam_parts(ml[...], vl[...], gradient[0:12, :])
    ml_out[...] = moment
    vl_out[...] = square
    share[0:12, :] = step
    for a in range(4):
        for b in range(4):
            top[4 * a + b : 4 * a + b + 1, :] = gradient[12 + a : 13 + a, 256 * b : 256 * b + 256]
    step, moment, square = adam_parts(mt[...], vt[...], top[:, 0:classes])
    mt_out[...] = moment
    vt_out[...] = square
    top[:, 0:classes] = step
    for a in range(4):
        for b in range(4):
            share[12 + a : 13 + a, 256 * b : 256 * b + 256] = top[4 * a + b : 4 * a + b + 1, :]
    everyone[me, rep] = share[...].astype(BF16)

    def tell(i):
        return pltpu.make_async_remote_copy(
            src_ref=everyone.at[me, rep], dst_ref=everyone.at[me, rep],
            send_sem=all_send.at[i], recv_sem=all_recv.at[i],
            device_id=(partner(i, chip, sign), rep), device_id_type=MESH,
        )

    def twin(i):
        came = partner(i, chip, -sign)
        return pltpu.make_async_remote_copy(
            src_ref=everyone.at[came, rep], dst_ref=everyone.at[came, rep],
            send_sem=twin_send.at[i], recv_sem=twin_recv.at[i],
            device_id=(me, other), device_id_type=MESH,
        )

    @pl.loop(1, STORES)
    def _(i):
        tell(i).start()

    twin(0).start()

    @pl.loop(1, STORES)
    def _(i):
        tell(i).wait_recv()
        twin(i).start()

    @pl.loop(0, STORES)
    def _(i):
        twin(i).wait()

        @pl.when(i > 0)
        def _():
            tell(i).wait_send()
            hand(i).wait_send()


def reduce_and_update(grads, first_low, second_low, first_top, second_top):
    tile = grads.shape[2:]
    vmem = pl.BlockSpec(memory_space=pltpu.VMEM)
    low = jax.ShapeDtypeStruct(first_low.shape, F32)
    top = jax.ShapeDtypeStruct(first_top.shape, F32)
    many = pltpu.SemaphoreType.DMA((STORES,))
    return pl.pallas_call(
        reduce_kernel,
        out_shape=(jax.ShapeDtypeStruct(grads.shape, BF16), low, low, top, top),
        in_specs=[vmem] * 5,
        out_specs=(vmem,) * 5,
        scratch_shapes=[
            pltpu.VMEM((STORES,) + tile, BF16),
            pltpu.VMEM((STORES,) + tile, BF16),
            pltpu.VMEM((STORES,) + tile, BF16),
            pltpu.VMEM(tile, F32),
            pltpu.VMEM((16, 256), F32),
            pltpu.SemaphoreType.DMA,
            pltpu.SemaphoreType.DMA,
            many, many, many, many, many, many,
        ],
        compiler_params=pltpu.CompilerParams(
            collective_id=1, has_side_effects=True, vmem_limit_bytes=32 << 20
        ),
    )(grads, first_low, second_low, first_top, second_top)


def finish_kernel(steps, wl, wt, wl_out, wt_out):
    wl_out[...] = wl[...] - dot(spread_low(), steps[...])
    classes = wt.shape[1]
    for m in range(2):
        rows = slice(256 * m, 256 * m + 256)
        top = jnp.zeros((256, 256), F32)
        for b in range(4):
            top = top + dot(spread_top(b), steps[rows, 256 * b : 256 * b + 256])
        wt_out[rows, :] = wt[rows, :] - top[:, 0:classes]


def finish(steps, weights_low, weights_top):
    rows, width = weights_low.shape
    tops, classes = weights_top.shape
    low = pl.BlockSpec((384, width), lambda i: (i, 0))
    top = pl.BlockSpec((512, classes), lambda i: (i, 0))
    return pl.pallas_call(
        finish_kernel,
        grid=(4,),
        out_shape=(
            jax.ShapeDtypeStruct((rows, width), F32),
            jax.ShapeDtypeStruct((tops, classes), F32),
        ),
        in_specs=[pl.BlockSpec((512, width), lambda i: (i, 0)), low, top],
        out_specs=(low, top),
        compiler_params=pltpu.CompilerParams(vmem_limit_bytes=32 << 20),
    )(steps, weights_low, weights_top)


def per_device(
    features,
    owners_near,
    slots_near,
    owners_far,
    slots_far,
    adjacency_low,
    adjacency_top,
    labels,
    weights_low,
    weights_top,
    first_low,
    second_low,
    first_top,
    second_top,
):
    near = adjacency_low.shape[0]
    owners = jnp.concatenate([owners_near[:, 0], owners_far[:, 0]])[None, :]
    slots = jnp.concatenate([slots_near[:, 0], slots_far[:, 0]])[None, :]
    entries = jnp.concatenate([adjacency_low, jnp.arange(near, dtype=jnp.int32)[:, None]], axis=1)
    x = fetch(owners, slots, entries, features)
    members = lax.axis_size(("store", "rep"))
    scale = 1.0 / (labels.shape[0] * members)
    logits, grads = local_step(x, weights_low, weights_top, adjacency_top, labels, scale)
    grads = grads.reshape(STORES, 2, 16, grads.shape[1])
    steps, new_first_low, new_second_low, new_first_top, new_second_top = reduce_and_update(
        grads, first_low, second_low, first_top, second_top
    )
    new_low, new_top = finish(steps.reshape(-1, grads.shape[3]), weights_low, weights_top)
    return (logits, new_low, new_first_low, new_second_low, new_top, new_first_top, new_second_top)


def solution(mesh):
    both = P(("store", "rep"), None)
    return jax.shard_map(
        per_device,
        mesh=mesh,
        in_specs=(
            P("store", None), both, both, both, both, both, both, P(("store", "rep")),
            P(), P(), both, both, both, both,
        ),
        out_specs=(both, P(), both, both, P(), both, both),
        check_vma=False,
    )
```

```python
import functools

import jax
import jax.numpy as jnp
from jax import lax
from jax.experimental import pallas as pl
from jax.experimental.pallas import tpu as pltpu
from jax.sharding import PartitionSpec as P

beta_one = 0.9
beta_two = 0.999
bias_one = 1.0 - 0.9**10
bias_two = 1.0 - 0.999**10
learn_rate = 0.01
adam_eps = 1e-08

MESH = pl.DeviceIdType.MESH
F32 = jnp.float32
BF16 = jnp.bfloat16
SIDE = 4
STORES = SIDE**3
CAP_NEAR = 16
CAP_FAR = 96
CAP = CAP_NEAR + CAP_FAR
STRIDE, UNSTRIDE = 37, 45


def iota(shape, dim):
    return lax.broadcasted_iota(jnp.int32, shape, dim)


def dot(a, b):
    return jnp.dot(a, b, preferred_element_type=F32)


def dot_nt(a, b):
    return lax.dot_general(a, b, (((1,), (1,)), ((), ())), preferred_element_type=F32)


def place():
    store = lax.axis_index("store")
    rep = lax.axis_index("rep")
    return (store // 16, lax.rem(store // 4, 4), lax.rem(store, 4)), rep, 1 - 2 * rep


def partner(slot, chip, sign):
    shift = lax.rem(slot * STRIDE, STORES)
    steps = (shift // 16, lax.rem(shift // 4, 4), lax.rem(shift, 4))
    x, y, z = [lax.rem(at + sign * step + SIDE, SIDE) for at, step in zip(chip, steps)]
    return (x * SIDE + y) * SIDE + z


def fetch_kernel(
    own, slots, adj, feat, out,
    table, cols, req_out, req_in, counts, send, recv, total, marks,
    ask_send, ask_recv, row_send, row_recv,
):
    chip, rep, sign = place()
    barrier = pltpu.get_barrier_semaphore()

    @pl.loop(1, STORES)
    def _(i):
        pl.semaphore_signal(
            barrier, inc=1, device_id=(partner(i, chip, sign), rep), device_id_type=MESH
        )

    table[...] = jnp.zeros_like(table)
    upper = (iota((256, 256), 0) < iota((256, 256), 1)).astype(BF16)
    base = jnp.zeros((STORES, 1), F32)
    high = jnp.zeros((STORES, 128), F32)
    low = jnp.zeros((STORES, 128), F32)
    near_blocks = adj.shape[0] // 256
    for b in range(own.shape[1] // 256):
        span = slice(256 * b, 256 * b + 256)
        if b == near_blocks:
            base = jnp.zeros((STORES, 1), F32)
        owner = own[:, span]
        wanted = slots[:, span]
        jx = (sign * (chip[0] - (owner >> 4))) & 3
        jy = (sign * (chip[1] - ((owner >> 2) & 3))) & 3
        jz = (sign * (chip[2] - (owner & 3))) & 3
        slot = (((jx * 16) + jy * 4 + jz) * UNSTRIDE) & 63
        owned = (iota((STORES, 256), 0) == slot).astype(F32)
        owned_bf = owned.astype(BF16)
        before = dot(owned_bf, upper) + base
        base = base + jnp.sum(owned, axis=1, keepdims=True)
        position = jnp.sum(owned * before, axis=0, keepdims=True)
        if b >= near_blocks:
            position = position + CAP_NEAR
        slot_f = slot.astype(F32)
        for half in range(2):
            part = slice(128 * half, 128 * half + 128)
            table[2 * b + half : 2 * b + half + 1, 0:128] = slot_f[:, part]
            table[2 * b + half : 2 * b + half + 1, 128:256] = position[:, part]
        placed = (iota((128, 256), 0) == position.astype(jnp.int32)).astype(F32)
        high = high + dot_nt(owned_bf, (placed * (wanted >> 6).astype(F32)).astype(BF16))
        low = low + dot_nt(owned_bf, (placed * (wanted & 63).astype(F32)).astype(BF16))
    requests = (high * 64.0 + low).astype(jnp.int32)
    for i in range(STORES):
        req_out[i] = requests[i : i + 1, :]
    req_in[0] = requests[0:1, :]

    pl.semaphore_wait(barrier, STORES - 1)

    def ask(i):
        return pltpu.make_async_remote_copy(
            src_ref=req_out.at[i], dst_ref=req_in.at[i],
            send_sem=ask_send.at[i], recv_sem=ask_recv.at[i],
            device_id=(partner(i, chip, -sign), rep), device_id_type=MESH,
        )

    def give(i):
        return pltpu.make_async_remote_copy(
            src_ref=send.at[i], dst_ref=recv.at[i],
            send_sem=row_send.at[i], recv_sem=row_recv.at[i],
            device_id=(partner(i, chip, sign), rep), device_id_type=MESH,
        )

    @pl.loop(1, STORES)
    def _(i):
        ask(i).start()

    table_bf = table[...].astype(BF16)
    near_rows = adj.shape[0]
    for k in range(adj.shape[1]):
        entry = adj[:, k : k + 1]
        row_mark = (iota((near_rows, 32), 1) == (entry >> 7)).astype(F32).astype(BF16)
        found = dot(row_mark, table_bf)
        column = found[:, 0:128] * float(CAP) + found[:, 128:256]
        lane = iota((near_rows, 128), 1) == (entry & 127)
        cols[:, k : k + 1] = jnp.sum(jnp.where(lane, column, 0.0), axis=1, keepdims=True)

    @pl.loop(1, STORES)
    def _(i):
        ask(i).wait()

    asked = jnp.concatenate(
        [req_in[i].astype(F32) for i in range(STORES)] + [jnp.zeros((64, 128), F32)], axis=0
    )
    asked = jnp.transpose(asked)[0:CAP, :]
    total[0:CAP, 0:128] = asked

    nodes = feat.shape[0]

    @pl.loop(0, STORES // 4)
    def _(g):
        for m in range(4):
            i = g * 4 + m
            lane = iota((CAP, 128), 1) == i
            row = jnp.sum(jnp.where(lane, total[0:CAP, 0:128], 0.0), axis=1, keepdims=True)
            row = row.astype(jnp.int32)
            for c in range(nodes // 512):
                marks[CAP * m : CAP * m + CAP, 512 * c : 512 * c + 512] = (
                    (iota((CAP, 512), 1) + 512 * c == row).astype(F32).astype(BF16)
                )
        for h in range(3):
            span = slice(256 * h, 256 * h + 256)
            rows = dot(marks[...], feat[:, span]).astype(BF16)
            for m in range(4):
                send[g * 4 + m, :, span] = rows[CAP * m : CAP * m + CAP]
        for m in range(4):
            i = g * 4 + m

            @pl.when(i > 0)
            def _():
                give(i).start()

    recv[0] = send[0]

    groups, width = counts.shape[0], counts.shape[2]

    @pl.loop(0, near_rows // 32)
    def _(r):
        rows = pl.ds(pl.multiple_of(r * 32, 32), 32)
        mine = pl.ds(pl.multiple_of(near_rows + r * 32, 32), 32)
        picked = cols[rows, :]
        for c in range(groups):
            lane = (iota((32, width), 1) + width * c).astype(F32)
            tally = jnp.zeros((32, width), F32)
            for k in range(15):
                tally = tally + jnp.where(lane == picked[:, k : k + 1], 1.0, 0.0)
            counts[c, rows, :] = tally.astype(BF16)
            counts[c, mine, :] = jnp.where(lane == picked[:, 15:16], 1.0, 0.0).astype(BF16)

    total[...] = jnp.zeros_like(total)

    @pl.loop(0, groups)
    def _(c):
        for m in range(STORES // groups):
            i = c * (STORES // groups) + m

            @pl.when(i > 0)
            def _():
                give(i).wait_recv()

        block = recv[pl.ds(c * (STORES // groups), STORES // groups)].reshape(width, recv.shape[2])
        for h in range(3):
            span = slice(256 * h, 256 * h + 256)
            total[:, span] += dot(counts[c], block[:, span])

    features = recv.shape[2]
    out[:, 0:features] = total[near_rows : 2 * near_rows, :].astype(BF16)
    out[:, features : 2 * features] = (total[0:near_rows, :] / 15.0).astype(BF16)

    @pl.loop(1, STORES)
    def _(i):
        give(i).wait_send()


def fetch(owners, slots, adjacency, features):
    near = adjacency.shape[0]
    width = features.shape[1]
    groups = 8
    vmem = pl.BlockSpec(memory_space=pltpu.VMEM)
    return pl.pallas_call(
        fetch_kernel,
        out_shape=jax.ShapeDtypeStruct((near, 2 * width), BF16),
        in_specs=[vmem] * 4,
        out_specs=vmem,
        scratch_shapes=[
            pltpu.VMEM((32, 256), F32),
            pltpu.VMEM((near, 16), F32),
            pltpu.VMEM((STORES, 1, 128), jnp.int32),
            pltpu.VMEM((STORES, 1, 128), jnp.int32),
            pltpu.VMEM((groups, 2 * near, STORES // groups * CAP), BF16),
            pltpu.VMEM((STORES, CAP, width), BF16),
            pltpu.VMEM((STORES, CAP, width), BF16),
            pltpu.VMEM((2 * near, width), F32),
            pltpu.VMEM((4 * CAP, features.shape[0]), BF16),
            pltpu.SemaphoreType.DMA((STORES,)),
            pltpu.SemaphoreType.DMA((STORES,)),
            pltpu.SemaphoreType.DMA((STORES,)),
            pltpu.SemaphoreType.DMA((STORES,)),
        ],
        compiler_params=pltpu.CompilerParams(
            collective_id=0, has_side_effects=True, vmem_limit_bytes=58 << 20
        ),
    )(owners, slots, adjacency, features)


def spread_low():
    row, column = iota((384, 512), 0), iota((384, 512), 1)
    inner = column & 15
    return ((inner < 12) & (row == 12 * (column >> 4) + inner)).astype(F32).astype(BF16)


def spread_low_t():
    column, row = iota((512, 384), 1), iota((512, 384), 0)
    inner = row & 15
    return ((inner < 12) & (column == 12 * (row >> 4) + inner)).astype(F32).astype(BF16)


def spread_top(b):
    row, column = iota((256, 256), 0), iota((256, 256), 1)
    inner = column & 15
    return (
        ((inner >= 12) & (row == (column & -16) + 4 * (inner - 12) + b)).astype(F32).astype(BF16)
    )


def spread_top_t(b):
    column, row = iota((256, 256), 1), iota((256, 256), 0)
    inner = row & 15
    return (
        ((inner >= 12) & (column == (row & -16) + 4 * (inner - 12) + b)).astype(F32).astype(BF16)
    )


def gelu_parts(v):
    root = 0.7978845608028654
    square = v * v
    t = jnp.tanh(root * (v + 0.044715 * (v * square)))
    gate = 0.5 * (1.0 + t)
    slope = gate + 0.5 * v * (1.0 - t * t) * (root * (1.0 + 3.0 * 0.044715 * square))
    return v * gate, slope


def step_part(scale, x, wl, wt, at, at_t, lab, logits_out, grads, wtb, hidden, slope, dpre, left):
    classes = wt.shape[1]
    width = wl.shape[1]
    seeds = at.shape[0]
    near = x.shape[0]
    wtb[...] = jnp.zeros_like(wtb)
    wtb[:, 0:classes] = wt[...].astype(BF16)
    for n in range(width // 256):
        span = slice(256 * n, 256 * n + 256)
        value, rise = gelu_parts(dot(x[...], wl[:, span].astype(BF16)))
        hidden[:, span] = value.astype(BF16)
        slope[:, span] = rise
    fan = at.shape[1]
    picks = jnp.zeros((seeds, near), F32)
    picks_t = jnp.zeros((near, seeds), F32)
    for k in range(fan):
        picks = picks + (iota((seeds, near), 1) == at[:, k : k + 1]).astype(F32)
        picks_t = picks_t + (iota((near, seeds), 0) == at_t[k : k + 1, :]).astype(F32)
    picks = picks.astype(BF16)
    picks_t = picks_t.astype(BF16)
    mean = (dot(picks, hidden[...]) / float(fan)).astype(BF16)
    own = hidden[0:seeds, :]
    logits = dot(own, wtb[0:width, :]) + dot(mean, wtb[width : 2 * width, :])
    logits_out[...] = logits[:, 0:classes]
    lane = iota(logits.shape, 1)
    powers = jnp.where(lane < classes, jnp.exp(logits), 0.0)
    chances = powers / jnp.sum(powers, axis=1, keepdims=True)
    targets = (lane == lab[...]).astype(F32)
    dlogits = ((chances - targets) * scale).astype(BF16)
    first = dot_nt(dlogits, wtb[0:width, :])
    second = dot_nt(dlogits, wtb[width : 2 * width, :]) / float(fan)
    second_high = second.astype(BF16)
    second_low = (second - second_high.astype(F32)).astype(BF16)
    for n in range(width // 256):
        span = slice(256 * n, 256 * n + 256)
        back = dot(picks_t, second_high[:, span]) + dot(picks_t, second_low[:, span])
        dpre[seeds:near, span] = (back[seeds:near] * slope[seeds:near, span]).astype(BF16)
        dpre[0:seeds, span] = ((back[0:seeds] + first[:, span]) * slope[0:seeds, span]).astype(BF16)
    low_t = spread_low_t()
    for m in range(x.shape[1] // 384):
        left[512 * m : 512 * m + 512, :] = dot_nt(low_t, x[:, 384 * m : 384 * m + 384]).astype(BF16)
    for b in range(width // 256):
        span = slice(256 * b, 256 * b + 256)
        top_t = spread_top_t(b)
        for m in range(2 * width // 256):
            source = own if m < width // 256 else mean
            at_col = 256 * (m % (width // 256))
            top_left = dot_nt(top_t, source[:, at_col : at_col + 256]).astype(BF16)
            rows = slice(256 * m, 256 * m + 256)
            block = dot(left[rows, :], dpre[:, span]) + dot(top_left, dlogits)
            grads[m // 2, 2 * (m % 2) : 2 * (m % 2) + 2, :, :, :, span] = block.astype(BF16).reshape(
                2, SIDE, 2, 16, 256
            )


def adam_parts(moment, square, gradient):
    moment_new = beta_one * moment + (1.0 - beta_one) * gradient
    square_new = beta_two * square + (1.0 - beta_two) * gradient * gradient
    update = moment_new / bias_one / (jnp.sqrt(square_new / bias_two) + adam_eps)
    return learn_rate * update, moment_new, square_new


SPANS = (slice(0, 384), slice(384, 768), slice(768, 1024))


def block_of(axes, fixed, tail):
    return tuple(fixed.get(axis, slice(None)) for axis in axes) + tail


def reduce_part(
    chip, rep, grads, ml, vl, mt, vt, everyone, ml_out, vl_out, mt_out, vt_out,
    pair, halves, got_one, sum_one, got_two, sum_two, got_three, share, top,
    pair_send, pair_recv, down_send, down_recv, up_send, up_recv, twin_send, twin_recv,
):
    other = 1 - rep
    classes = mt.shape[1]
    every = slice(None)

    def copy(src, dst, send_sem, recv_sem, at, core):
        return pltpu.make_async_remote_copy(
            src_ref=src, dst_ref=dst, send_sem=send_sem, recv_sem=recv_sem,
            device_id=((at[0] * SIDE + at[1]) * SIDE + at[2], core), device_id_type=MESH,
        )

    def moved(axis, step):
        return [lax.rem(c + step, SIDE) if n == axis else c for n, c in enumerate(chip)]

    swaps = []
    for c, span in enumerate(SPANS):
        swaps.append(copy(
            grads.at[:, :, :, other, :, span], pair.at[:, :, :, :, span],
            pair_send.at[c], pair_recv.at[c], chip, other,
        ))
        swaps[c].start()
    sent = list(swaps)
    got = (got_one, got_two, got_three)
    waiting = []
    for c, span in enumerate(SPANS):
        swaps[c].wait_recv()

        @pl.loop(0, SIDE)
        def _(x):
            for y in range(SIDE):
                for z in range(SIDE):
                    halves[x, y, z, :, span] = (
                        grads[x, y, z, rep, :, span].astype(F32) + pair[x, y, z, :, span].astype(F32)
                    ).astype(BF16)

        axes, first = (0, 1, 2), c
        copies = []
        for k in range(1, SIDE):
            to = moved(first, k)
            copies.append(copy(
                halves.at[block_of(axes, {first: to[first]}, (every, span))],
                got_one.at[k - 1, :, :, :, span],
                down_send.at[0, c, k - 1], down_recv.at[0, c, k - 1], to, rep,
            ))
            copies[-1].start()
        sent += copies
        waiting.append(copies)
    following = []
    for c, span in enumerate(SPANS):
        first, second = c, (c + 1) % 3
        left = tuple(n for n in range(3) if n != first)
        for made in waiting[c]:
            made.wait_recv()
        for a in range(SIDE):
            for b in range(SIDE):
                spot = {left[0]: a, left[1]: b, first: chip[first]}
                total = halves[block_of((0, 1, 2), spot, (every, span))].astype(F32)
                for k in range(1, SIDE):
                    total = total + got_one[k - 1, a, b, :, span].astype(F32)
                sum_one[a, b, :, span] = total.astype(BF16)
        copies = []
        for k in range(1, SIDE):
            to = moved(second, k)
            copies.append(copy(
                sum_one.at[block_of(left, {second: to[second]}, (every, span))],
                got_two.at[k - 1, :, :, span],
                down_send.at[1, c, k - 1], down_recv.at[1, c, k - 1], to, rep,
            ))
            copies[-1].start()
        sent += copies
        following.append(copies)
    waiting, following = following, []
    for c, span in enumerate(SPANS):
        first, second, third = c, (c + 1) % 3, (c + 2) % 3
        left = tuple(n for n in range(3) if n != first)
        for made in waiting[c]:
            made.wait_recv()
        for a in range(SIDE):
            spot = {third: a, second: chip[second]}
            total = sum_one[block_of(left, spot, (every, span))].astype(F32)
            for k in range(1, SIDE):
                total = total + got_two[k - 1, a, :, span].astype(F32)
            sum_two[a, :, span] = total.astype(BF16)
        copies = []
        for k in range(1, SIDE):
            to = moved(third, k)
            copies.append(copy(
                sum_two.at[to[third], :, span], got_three.at[k - 1, :, span],
                down_send.at[2, c, k - 1], down_recv.at[2, c, k - 1], to, rep,
            ))
            copies[-1].start()
        sent += copies
        following.append(copies)
    for c, span in enumerate(SPANS):
        for made in following[c]:
            made.wait_recv()
        total = sum_two[chip[(c + 2) % 3], :, span].astype(F32)
        for k in range(1, SIDE):
            total = total + got_three[k - 1, :, span].astype(F32)
        share[:, span] = total

    step, moment, square = adam_parts(ml[...], vl[...], share[0:12, :])
    ml_out[...] = moment
    vl_out[...] = square
    for a in range(4):
        for b in range(4):
            top[4 * a + b : 4 * a + b + 1, :] = share[12 + a : 13 + a, 256 * b : 256 * b + 256]
    share[0:12, :] = step
    step, moment, square = adam_parts(mt[...], vt[...], top[:, 0:classes])
    mt_out[...] = moment
    vt_out[...] = square
    top[:, 0:classes] = step
    for a in range(4):
        for b in range(4):
            share[12 + a : 13 + a, 256 * b : 256 * b + 256] = top[4 * a + b : 4 * a + b + 1, :]
    everyone[chip[0], chip[1], chip[2], rep] = share[...].astype(BF16)

    waiting = [[] for span in SPANS]
    twins = []
    for level in range(4):
        for c, span in enumerate(SPANS):
            order = ((c + 2) % 3, (c + 1) % 3, c)
            for made in waiting[c]:
                made.wait_recv()
            if level < 3:
                spot = {n: chip[n] for n in order[level:]}
                block = everyone.at[block_of((0, 1, 2), spot, (rep, every, span))]
                waiting[c] = []
                for k in range(1, SIDE):
                    waiting[c].append(copy(
                        block, block, up_send.at[level, c, k - 1], up_recv.at[level, c, k - 1],
                        moved(order[level], k), rep,
                    ))
                    waiting[c][-1].start()
                sent += waiting[c]
            if level >= 2:
                for k in range(1 if level == 3 else 0, SIDE if level == 3 else 1):
                    spot = {c: lax.rem(chip[c] + SIDE - k, SIDE)}
                    block = everyone.at[block_of((0, 1, 2), spot, (rep, every, span))]
                    twins.append(copy(
                        block, block, twin_send.at[c, k], twin_recv.at[c, k], chip, other
                    ))
                    twins[-1].start()
    for made in twins:
        made.wait()
    for made in sent:
        made.wait_send()


def train_kernel(
    scale, x, wl, wt, at, at_t, lab, ml, vl, mt, vt,
    logits_out, everyone, ml_out, vl_out, mt_out, vt_out,
    wtb, hidden, slope, dpre, left, grads, *scratch,
):
    chip, rep, _ = place()
    barrier = pltpu.get_barrier_semaphore()
    for axis in range(3):
        for k in range(1, SIDE):
            at_k = [lax.rem(c + k, SIDE) if n == axis else c for n, c in enumerate(chip)]
            to = (at_k[0] * SIDE + at_k[1]) * SIDE + at_k[2]
            pl.semaphore_signal(barrier, inc=1, device_id=(to, rep), device_id_type=MESH)
    pl.semaphore_signal(
        barrier, inc=1, device_id=(lax.axis_index("store"), 1 - rep), device_id_type=MESH
    )
    step_part(scale, x, wl, wt, at, at_t, lab, logits_out, grads, wtb, hidden, slope, dpre, left)
    pl.semaphore_wait(barrier, 10)
    reduce_part(
        chip, rep, grads, ml, vl, mt, vt, everyone, ml_out, vl_out, mt_out, vt_out, *scratch
    )


def train(x, weights_low, weights_top, adjacency_top, labels, scale, ml, vl, mt, vt):
    near = x.shape[0]
    seeds, fan = adjacency_top.shape
    width = weights_low.shape[1]
    cube = (SIDE, SIDE, SIDE)
    tile = (16, width)
    vmem = pl.BlockSpec(memory_space=pltpu.VMEM)
    low = jax.ShapeDtypeStruct(ml.shape, F32)
    top = jax.ShapeDtypeStruct(mt.shape, F32)
    hops = pltpu.SemaphoreType.DMA((3, 3, 3))
    return pl.pallas_call(
        functools.partial(train_kernel, scale),
        out_shape=(
            jax.ShapeDtypeStruct((seeds, weights_top.shape[1]), F32),
            jax.ShapeDtypeStruct(cube + (2,) + tile, BF16),
            low, low, top, top,
        ),
        in_specs=[vmem] * 10,
        out_specs=(vmem,) * 6,
        scratch_shapes=[
            pltpu.VMEM((2 * width, 256), BF16),
            pltpu.VMEM((near, width), BF16),
            pltpu.VMEM((near, width), F32),
            pltpu.VMEM((near, width), BF16),
            pltpu.VMEM((2 * width, near), BF16),
            pltpu.VMEM(cube + (2,) + tile, BF16),
            pltpu.VMEM(cube + tile, BF16),
            pltpu.VMEM(cube + tile, BF16),
            pltpu.VMEM((SIDE - 1, SIDE, SIDE) + tile, BF16),
            pltpu.VMEM((SIDE, SIDE) + tile, BF16),
            pltpu.VMEM((SIDE - 1, SIDE) + tile, BF16),
            pltpu.VMEM((SIDE,) + tile, BF16),
            pltpu.VMEM((SIDE - 1,) + tile, BF16),
            pltpu.VMEM(tile, F32),
            pltpu.VMEM((16, 256), F32),
            pltpu.SemaphoreType.DMA((3,)),
            pltpu.SemaphoreType.DMA((3,)),
            hops, hops, hops, hops,
            pltpu.SemaphoreType.DMA((3, SIDE)),
            pltpu.SemaphoreType.DMA((3, SIDE)),
        ],
        compiler_params=pltpu.CompilerParams(
            collective_id=1, has_side_effects=True, vmem_limit_bytes=50 << 20
        ),
    )(
        x, weights_low, weights_top, adjacency_top, adjacency_top.T, labels[:, None],
        ml, vl, mt, vt,
    )


def finish_kernel(steps, wl, wt, wl_out, wt_out):
    wl_out[...] = wl[...] - dot(spread_low(), steps[...])
    classes = wt.shape[1]
    for m in range(2):
        rows = slice(256 * m, 256 * m + 256)
        top = jnp.zeros((256, 256), F32)
        for b in range(4):
            top = top + dot(spread_top(b), steps[rows, 256 * b : 256 * b + 256])
        wt_out[rows, :] = wt[rows, :] - top[:, 0:classes]


def finish(steps, weights_low, weights_top):
    rows, width = weights_low.shape
    tops, classes = weights_top.shape
    low = pl.BlockSpec((384, width), lambda i: (i, 0))
    top = pl.BlockSpec((512, classes), lambda i: (i, 0))
    return pl.pallas_call(
        finish_kernel,
        grid=(4,),
        out_shape=(
            jax.ShapeDtypeStruct((rows, width), F32),
            jax.ShapeDtypeStruct((tops, classes), F32),
        ),
        in_specs=[pl.BlockSpec((512, width), lambda i: (i, 0)), low, top],
        out_specs=(low, top),
        compiler_params=pltpu.CompilerParams(vmem_limit_bytes=32 << 20),
    )(steps, weights_low, weights_top)


def per_device(
    features,
    owners_near,
    slots_near,
    owners_far,
    slots_far,
    adjacency_low,
    adjacency_top,
    labels,
    weights_low,
    weights_top,
    first_low,
    second_low,
    first_top,
    second_top,
):
    near = adjacency_low.shape[0]
    owners = jnp.concatenate([owners_near[:, 0], owners_far[:, 0]])[None, :]
    slots = jnp.concatenate([slots_near[:, 0], slots_far[:, 0]])[None, :]
    entries = jnp.concatenate([adjacency_low, jnp.arange(near, dtype=jnp.int32)[:, None]], axis=1)
    x = fetch(owners, slots, entries, features)
    members = lax.axis_size(("store", "rep"))
    scale = 1.0 / (labels.shape[0] * members)
    logits, steps, new_first_low, new_second_low, new_first_top, new_second_top = train(
        x, weights_low, weights_top, adjacency_top, labels, scale,
        first_low, second_low, first_top, second_top,
    )
    new_low, new_top = finish(steps.reshape(-1, steps.shape[-1]), weights_low, weights_top)
    return (logits, new_low, new_first_low, new_second_low, new_top, new_first_top, new_second_top)


def solution(mesh):
    both = P(("store", "rep"), None)
    return jax.shard_map(
        per_device,
        mesh=mesh,
        in_specs=(
            P("store", None), both, both, both, both, both, both, P(("store", "rep")),
            P(), P(), both, both, both, both,
        ),
        out_specs=(both, P(), both, both, P(), both, both),
        check_vma=False,
    )
```

```python
import functools

import jax
import jax.numpy as jnp
from jax import lax
from jax.experimental import pallas as pl
from jax.experimental.pallas import tpu as pltpu
from jax.sharding import PartitionSpec as P

beta_one = 0.9
beta_two = 0.999
bias_one = 1.0 - 0.9**10
bias_two = 1.0 - 0.999**10
learn_rate = 0.01
adam_eps = 1e-08

MESH = pl.DeviceIdType.MESH
F32 = jnp.float32
BF16 = jnp.bfloat16
SIDE = 4
STORES = SIDE**3
CAP_NEAR = 16
CAP_FAR = 96
CAP = CAP_NEAR + CAP_FAR


def iota(shape, dim):
    return lax.broadcasted_iota(jnp.int32, shape, dim)


def dot(a, b):
    return jnp.dot(a, b, preferred_element_type=F32)


def dot_nt(a, b):
    return lax.dot_general(a, b, (((1,), (1,)), ((), ())), preferred_element_type=F32)


def place():
    store = lax.axis_index("store")
    return (store // 16, lax.rem(store // 4, 4), lax.rem(store, 4)), lax.axis_index("rep")


def at(chip):
    return (chip[0] * SIDE + chip[1]) * SIDE + chip[2]


def moved(chip, axis, step):
    return [lax.rem(c + step, SIDE) if n == axis else c for n, c in enumerate(chip)]


def partner(shift, chip, sign):
    steps = (shift // 16, lax.rem(shift // 4, 4), lax.rem(shift, 4))
    return at([lax.rem(c + sign * step + SIDE, SIDE) for c, step in zip(chip, steps)])


def routes():
    load = [[0] * 3 for _ in range(3)]
    found = {}
    by_hops = {1: [], 2: [], 3: []}
    for shift in range(1, STORES):
        steps = (shift // 16, shift // 4 % 4, shift % 4)
        by_hops[sum(step != 0 for step in steps)].append((shift, steps))
    for hops in (3, 2, 1):
        for shift, steps in by_hops[hops]:
            options = [
                [axis for axis in order if steps[axis]]
                for order in ((0, 1, 2), (1, 2, 0), (2, 0, 1), (0, 2, 1), (2, 1, 0), (1, 0, 2))
            ]
            cost = lambda order: sum(
                load[h][axis] * min(steps[axis], SIDE - steps[axis]) * (3 - h)
                for h, axis in enumerate(order)
            )
            order = min(options, key=cost)
            for h, axis in enumerate(order):
                load[h][axis] += min(steps[axis], SIDE - steps[axis])
            found[shift] = [(axis, steps[axis]) for axis in order]
    return found, *([shift for shift, _ in by_hops[hops]] for hops in (3, 2, 1))


ROUTES, THREE, TWO, ONE = routes()
LEAVE = THREE + TWO + ONE + [0]
ARRIVE = [0] + ONE + [shift for both in zip(TWO, THREE) for shift in both]
SEGMENTS = (1, 2, 4, 9)
GROUPS = 8


def fetch_kernel(
    own_near, slot_near, own_far, slot_far, adj, spots, feat, out,
    table, cols, chosen, req_out, req_in, asked, counts, selves, send, relay_one, relay_two, recv,
    total, marks,
    ask_send, ask_recv, send_one, send_two, send_three, recv_one, recv_two, recv_three,
):
    chip, rep = place()
    barrier = pltpu.get_barrier_semaphore()

    @pl.loop(1, STORES)
    def _(shift):
        pl.semaphore_signal(
            barrier, inc=1, device_id=(partner(shift, chip, 1), rep), device_id_type=MESH
        )

    table[...] = jnp.zeros_like(table)
    upper = (iota((256, 256), 0) < iota((256, 256), 1)).astype(BF16)
    base = jnp.zeros((STORES, 1), F32)
    high = jnp.zeros((STORES, 128), F32)
    low = jnp.zeros((STORES, 128), F32)
    near_rows = own_near.shape[1]
    near_blocks = near_rows // 256
    spot = spots[:, 0:1]
    for b in range(near_blocks + own_far.shape[1] // 256):
        far = b >= near_blocks
        if b == near_blocks:
            base = jnp.zeros((STORES, 1), F32)
        first = 256 * (b - near_blocks if far else b)
        owner = (own_far if far else own_near)[:, first : first + 256]
        wanted = (slot_far if far else slot_near)[:, first : first + 256]
        jx = (chip[0] - (owner >> 4)) & 3
        jy = (chip[1] - ((owner >> 2) & 3)) & 3
        jz = (chip[2] - (owner & 3)) & 3
        shift = jx * 16 + jy * 4 + jz
        owned = (iota((STORES, 256), 0) == shift).astype(F32)
        owned_bf = owned.astype(BF16)
        before = dot(owned_bf, upper) + base
        base = base + jnp.sum(owned, axis=1, keepdims=True)
        position = jnp.sum(owned * before, axis=0, keepdims=True)
        if far:
            position = position + CAP_NEAR
        arrival = jnp.sum(owned * spot, axis=0, keepdims=True)
        for half in range(2):
            part = slice(128 * half, 128 * half + 128)
            table[2 * b + half : 2 * b + half + 1, 0:128] = arrival[:, part]
            table[2 * b + half : 2 * b + half + 1, 128:256] = position[:, part]
        placed = (iota((128, 256), 0) == position.astype(jnp.int32)).astype(F32)
        high = high + dot_nt(owned_bf, (placed * (wanted >> 6).astype(F32)).astype(BF16))
        low = low + dot_nt(owned_bf, (placed * (wanted & 63).astype(F32)).astype(BF16))
    requests = (high * 64.0 + low).astype(jnp.int32)
    for shift in range(STORES):
        req_out[shift] = requests[shift : shift + 1, :]
    req_in[0] = requests[0:1, :]

    pl.semaphore_wait(barrier, STORES - 1)

    def ask(shift):
        return pltpu.make_async_remote_copy(
            src_ref=req_out.at[shift], dst_ref=req_in.at[shift],
            send_sem=ask_send.at[shift], recv_sem=ask_recv.at[shift],
            device_id=(partner(shift, chip, -1), rep), device_id_type=MESH,
        )

    @pl.loop(1, STORES)
    def _(shift):
        ask(shift).start()

    table_t = jnp.transpose(table[...]).astype(BF16)
    fan = adj.shape[0]
    cols[...] = jnp.zeros_like(cols)
    for k in range(fan + 1):
        entry = adj[k : k + 1, :] if k < fan else iota((1, near_rows), 1)
        row_mark = (iota((128, near_rows), 0) == (entry >> 7)).astype(F32).astype(BF16)
        found = dot(table_t, row_mark)
        column = found[0:128] * float(CAP if k < fan else CAP_NEAR) + found[128:256]
        picked = iota((128, near_rows), 0) == (entry & 127)
        cols[k : k + 1, :] = jnp.sum(jnp.where(picked, column, 0.0), axis=0, keepdims=True)
    for c in range(near_rows // 128):
        block = slice(128 * c, 128 * c + 128)
        chosen[block, :] = jnp.transpose(cols[:, block])

    @pl.loop(1, STORES)
    def _(shift):
        ask(shift).wait()

    lists = jnp.concatenate(
        [req_in[shift].astype(F32) for shift in LEAVE] + [jnp.zeros((64, 128), F32)], axis=0
    )
    asked[...] = jnp.transpose(lists)[0:CAP, :]

    hops = {}

    def go(shift, hop):
        route = ROUTES[shift]
        if hop == 0:
            src = send.at[LEAVE.index(shift)]
        elif hop == 1:
            src = relay_one.at[LEAVE.index(shift)]
        else:
            src = relay_two.at[LEAVE.index(shift)]
        if hop == len(route) - 1:
            dst = recv.at[ARRIVE.index(shift)]
        elif hop == 0:
            dst = relay_one.at[LEAVE.index(shift)]
        else:
            dst = relay_two.at[LEAVE.index(shift)]
        hops[shift, hop] = pltpu.make_async_remote_copy(
            src_ref=src, dst_ref=dst,
            send_sem=(send_one, send_two, send_three)[hop].at[shift],
            recv_sem=(recv_one, recv_two, recv_three)[hop].at[shift],
            device_id=(at(moved(chip, *route[hop])), rep), device_id_type=MESH,
        )
        hops[shift, hop].start()

    nodes = feat.shape[0]

    def pick(g):
        for m in range(4):
            lane = iota((CAP, 128), 1) == g * 4 + m
            row = jnp.sum(jnp.where(lane, asked[...], 0.0), axis=1, keepdims=True)
            row = row.astype(jnp.int32)
            for c in range(nodes // 512):
                marks[CAP * m : CAP * m + CAP, 512 * c : 512 * c + 512] = (
                    (iota((CAP, 512), 1) + 512 * c == row).astype(F32).astype(BF16)
                )
        for h in range(3):
            span = slice(256 * h, 256 * h + 256)
            rows = dot(marks[...], feat[:, span]).astype(BF16)
            for m in range(4):
                send[g * 4 + m, :, span] = rows[CAP * m : CAP * m + CAP]

    begin = 0
    for size in SEGMENTS:
        pl.loop(begin, begin + size)(pick)
        for shift in LEAVE[4 * begin : 4 * (begin + size)]:
            if shift and (shift in THREE or shift in TWO):
                go(shift, 0)
        begin += size
    recv[0] = send[STORES - 1]
    for shift in THREE:
        hops[shift, 0].wait_recv()
        go(shift, 1)
    for shift in ONE:
        go(shift, 0)

    width = counts.shape[2]

    @pl.loop(0, near_rows // 32)
    def _(r):
        rows = pl.ds(pl.multiple_of(r * 32, 32), 32)
        picked = chosen[rows, :]
        for c in range(GROUPS):
            lane = (iota((32, width), 1) + width * c).astype(F32)
            tally = jnp.zeros((32, width), F32)
            for k in range(fan):
                tally = tally + jnp.where(lane == picked[:, k : k + 1], 1.0, 0.0)
            counts[c, rows, :] = tally.astype(BF16)
            lane = (iota((32, 128), 1) + 128 * c).astype(F32)
            selves[c, rows, :] = jnp.where(lane == picked[:, fan : fan + 1], 1.0, 0.0).astype(BF16)

    for shift in TWO:
        hops[shift, 0].wait_recv()
        go(shift, 1)
    for shift in THREE:
        hops[shift, 1].wait_recv()
        go(shift, 2)

    features = recv.shape[2]
    many = STORES // GROUPS
    for c in range(GROUPS):
        for shift in ARRIVE[many * c : many * (c + 1)]:
            if shift:
                hops[shift, len(ROUTES[shift]) - 1].wait_recv()
        for h in range(3):
            span = slice(256 * h, 256 * h + 256)
            block = recv[many * c : many * (c + 1), :, span].reshape(width, 256)
            nears = recv[many * c : many * (c + 1), 0:CAP_NEAR, span].reshape(128, 256)
            sums = dot(counts[c], block)
            same = dot(selves[c], nears).astype(BF16)
            if c:
                sums = sums + total[:, span]
                same = same + out[:, span]
            out[:, span] = same
            if c < GROUPS - 1:
                total[:, span] = sums
            else:
                out[:, features + 256 * h : features + 256 * h + 256] = (
                    sums / float(fan)
                ).astype(BF16)
    for made in hops.values():
        made.wait_send()


def fetch(owners_near, slots_near, owners_far, slots_far, adjacency, features):
    near = adjacency.shape[1]
    width = features.shape[1]
    vmem = pl.BlockSpec(memory_space=pltpu.VMEM)
    spots = jnp.array([[ARRIVE.index(shift)] * 128 for shift in range(STORES)], F32)
    rows = (CAP, width)
    many = pltpu.SemaphoreType.DMA((STORES,))
    return pl.pallas_call(
        fetch_kernel,
        out_shape=jax.ShapeDtypeStruct((near, 2 * width), BF16),
        in_specs=[vmem] * 7,
        out_specs=vmem,
        scratch_shapes=[
            pltpu.VMEM((128, 256), F32),
            pltpu.VMEM((128, near), F32),
            pltpu.VMEM((near, 128), F32),
            pltpu.VMEM((STORES, 1, 128), jnp.int32),
            pltpu.VMEM((STORES, 1, 128), jnp.int32),
            pltpu.VMEM((CAP, 128), F32),
            pltpu.VMEM((GROUPS, near, STORES // GROUPS * CAP), BF16),
            pltpu.VMEM((GROUPS, near, 128), BF16),
            pltpu.VMEM((STORES,) + rows, BF16),
            pltpu.VMEM((len(THREE) + len(TWO),) + rows, BF16),
            pltpu.VMEM((len(THREE),) + rows, BF16),
            pltpu.VMEM((STORES,) + rows, BF16),
            pltpu.VMEM((near, width), F32),
            pltpu.VMEM((4 * CAP, features.shape[0]), BF16),
            many, many, many, many, many, many, many, many,
        ],
        compiler_params=pltpu.CompilerParams(
            collective_id=0, has_side_effects=True, vmem_limit_bytes=60 << 20
        ),
    )(owners_near, slots_near, owners_far, slots_far, adjacency, spots, features)


def spread_low():
    row, column = iota((384, 512), 0), iota((384, 512), 1)
    inner = column & 15
    return ((inner < 12) & (row == 12 * (column >> 4) + inner)).astype(F32).astype(BF16)


def spread_low_t():
    column, row = iota((512, 384), 1), iota((512, 384), 0)
    inner = row & 15
    return ((inner < 12) & (column == 12 * (row >> 4) + inner)).astype(F32).astype(BF16)


def spread_top(b):
    row, column = iota((256, 256), 0), iota((256, 256), 1)
    inner = column & 15
    return (
        ((inner >= 12) & (row == (column & -16) + 4 * (inner - 12) + b)).astype(F32).astype(BF16)
    )


def spread_top_t(b):
    column, row = iota((256, 256), 1), iota((256, 256), 0)
    inner = row & 15
    return (
        ((inner >= 12) & (column == (row & -16) + 4 * (inner - 12) + b)).astype(F32).astype(BF16)
    )


def gelu_parts(v):
    root = 0.7978845608028654
    square = v * v
    t = jnp.tanh(root * (v + 0.044715 * (v * square)))
    gate = 0.5 * (1.0 + t)
    slope = gate + 0.5 * v * (1.0 - t * t) * (root * (1.0 + 3.0 * 0.044715 * square))
    return v * gate, slope


def step_part(scale, x, wl, wt_t, at_t, lab, logits_out, grads, wtb, hidden, slope, dpre, left):
    classes = wt_t.shape[0]
    width = wl.shape[1]
    fan, seeds = at_t.shape
    near = x.shape[0]
    wtb[...] = jnp.zeros_like(wtb)
    wtb[0:classes, :] = wt_t[...].astype(BF16)
    for n in range(width // 256):
        span = slice(256 * n, 256 * n + 256)
        value, rise = gelu_parts(dot(x[...], wl[:, span].astype(BF16)))
        hidden[:, span] = value.astype(BF16)
        slope[:, span] = rise
    picks_t = jnp.zeros((near, seeds), F32)
    for k in range(fan):
        picks_t = picks_t + (iota((near, seeds), 0) == at_t[k : k + 1, :]).astype(F32)
    picks = jnp.transpose(picks_t).astype(BF16)
    picks_t = picks_t.astype(BF16)
    mean = (dot(picks, hidden[...]) / float(fan)).astype(BF16)
    own = hidden[0:seeds, :]
    logits = dot_nt(wtb[:, 0:width], own) + dot_nt(wtb[:, width : 2 * width], mean)
    logits_out[...] = logits[0:classes]
    line = iota(logits.shape, 0)
    powers = jnp.where(line < classes, jnp.exp(logits), 0.0)
    chances = powers / jnp.sum(powers, axis=0, keepdims=True)
    targets = (line == lab[...]).astype(F32)
    dlogits = jnp.transpose((chances - targets) * scale).astype(BF16)
    first = dot(dlogits, wtb[:, 0:width])
    second = dot(dlogits, wtb[:, width : 2 * width]) / float(fan)
    second_high = second.astype(BF16)
    second_low = (second - second_high.astype(F32)).astype(BF16)
    for n in range(width // 256):
        span = slice(256 * n, 256 * n + 256)
        back = dot(picks_t, second_high[:, span]) + dot(picks_t, second_low[:, span])
        dpre[seeds:near, span] = (back[seeds:near] * slope[seeds:near, span]).astype(BF16)
        dpre[0:seeds, span] = ((back[0:seeds] + first[:, span]) * slope[0:seeds, span]).astype(BF16)
    low_t = spread_low_t()
    for m in range(x.shape[1] // 384):
        left[512 * m : 512 * m + 512, :] = dot_nt(low_t, x[:, 384 * m : 384 * m + 384]).astype(BF16)
    for b in range(width // 256):
        span = slice(256 * b, 256 * b + 256)
        top_t = spread_top_t(b)
        for m in range(2 * width // 256):
            source = own if m < width // 256 else mean
            at_col = 256 * (m % (width // 256))
            top_left = dot_nt(top_t, source[:, at_col : at_col + 256]).astype(BF16)
            rows = slice(256 * m, 256 * m + 256)
            block = dot(left[rows, :], dpre[:, span]) + dot(top_left, dlogits)
            grads[m // 2, 2 * (m % 2) : 2 * (m % 2) + 2, :, :, :, span] = block.astype(BF16).reshape(
                2, SIDE, 2, 16, 256
            )


def adam_parts(moment, square, gradient):
    moment_new = beta_one * moment + (1.0 - beta_one) * gradient
    square_new = beta_two * square + (1.0 - beta_two) * gradient * gradient
    update = moment_new / bias_one / (jnp.sqrt(square_new / bias_two) + adam_eps)
    return learn_rate * update, moment_new, square_new


SPANS = (slice(0, 384), slice(384, 768), slice(768, 1024))


def top_rows(share, top):
    for a in range(4):
        for b in range(4):
            top[4 * a + b : 4 * a + b + 1, :] = share[12 + a : 13 + a, 256 * b : 256 * b + 256]


def block_of(axes, fixed, tail):
    return tuple(fixed.get(axis, slice(None)) for axis in axes) + tail


def reduce_part(
    chip, rep, grads, ml, vl, mt, vt, everyone, gradient_out,
    pair, halves, got_one, sum_one, got_two, sum_two, got_three, share, top,
    pair_send, pair_recv, down_send, down_recv, up_send, up_recv, twin_send, twin_recv,
):
    other = 1 - rep
    classes = mt.shape[1]
    every = slice(None)

    def copy(src, dst, send_sem, recv_sem, to, core):
        return pltpu.make_async_remote_copy(
            src_ref=src, dst_ref=dst, send_sem=send_sem, recv_sem=recv_sem,
            device_id=(at(to), core), device_id_type=MESH,
        )

    swaps = []
    for c, span in enumerate(SPANS):
        swaps.append(copy(
            grads.at[:, :, :, other, :, span], pair.at[:, :, :, :, span],
            pair_send.at[c], pair_recv.at[c], chip, other,
        ))
        swaps[c].start()
    sent = list(swaps)
    got = (got_one, got_two, got_three)
    waiting = []
    for c, span in enumerate(SPANS):
        swaps[c].wait_recv()

        @pl.loop(0, SIDE)
        def _(x):
            for y in range(SIDE):
                for z in range(SIDE):
                    halves[x, y, z, :, span] = (
                        grads[x, y, z, rep, :, span].astype(F32) + pair[x, y, z, :, span].astype(F32)
                    ).astype(BF16)

        axes, first = (0, 1, 2), c
        copies = []
        for k in range(1, SIDE):
            to = moved(chip, first, k)
            copies.append(copy(
                halves.at[block_of(axes, {first: to[first]}, (every, span))],
                got_one.at[k - 1, :, :, :, span],
                down_send.at[0, c, k - 1], down_recv.at[0, c, k - 1], to, rep,
            ))
            copies[-1].start()
        sent += copies
        waiting.append(copies)
    following = []
    for c, span in enumerate(SPANS):
        first, second = c, (c + 1) % 3
        left = tuple(n for n in range(3) if n != first)
        for made in waiting[c]:
            made.wait_recv()
        for a in range(SIDE):
            for b in range(SIDE):
                spot = {left[0]: a, left[1]: b, first: chip[first]}
                total = halves[block_of((0, 1, 2), spot, (every, span))].astype(F32)
                for k in range(1, SIDE):
                    total = total + got_one[k - 1, a, b, :, span].astype(F32)
                sum_one[a, b, :, span] = total.astype(BF16)
        copies = []
        for k in range(1, SIDE):
            to = moved(chip, second, k)
            copies.append(copy(
                sum_one.at[block_of(left, {second: to[second]}, (every, span))],
                got_two.at[k - 1, :, :, span],
                down_send.at[1, c, k - 1], down_recv.at[1, c, k - 1], to, rep,
            ))
            copies[-1].start()
        sent += copies
        following.append(copies)
    waiting, following = following, []
    for c, span in enumerate(SPANS):
        first, second, third = c, (c + 1) % 3, (c + 2) % 3
        left = tuple(n for n in range(3) if n != first)
        for made in waiting[c]:
            made.wait_recv()
        for a in range(SIDE):
            spot = {third: a, second: chip[second]}
            total = sum_one[block_of(left, spot, (every, span))].astype(F32)
            for k in range(1, SIDE):
                total = total + got_two[k - 1, a, :, span].astype(F32)
            sum_two[a, :, span] = total.astype(BF16)
        copies = []
        for k in range(1, SIDE):
            to = moved(chip, third, k)
            copies.append(copy(
                sum_two.at[to[third], :, span], got_three.at[k - 1, :, span],
                down_send.at[2, c, k - 1], down_recv.at[2, c, k - 1], to, rep,
            ))
            copies[-1].start()
        sent += copies
        following.append(copies)
    for c, span in enumerate(SPANS):
        for made in following[c]:
            made.wait_recv()
        total = sum_two[chip[(c + 2) % 3], :, span].astype(F32)
        for k in range(1, SIDE):
            total = total + got_three[k - 1, :, span].astype(F32)
        share[:, span] = total

    gradient_out[...] = share[...]
    top_rows(share, top)
    share[0:12, :] = adam_parts(ml[...], vl[...], share[0:12, :])[0]
    step = adam_parts(mt[...], vt[...], top[:, 0:classes])[0]
    top[:, 0:classes] = step
    for a in range(4):
        for b in range(4):
            share[12 + a : 13 + a, 256 * b : 256 * b + 256] = top[4 * a + b : 4 * a + b + 1, :]
    everyone[chip[0], chip[1], chip[2], rep] = share[...].astype(BF16)

    waiting = [[] for span in SPANS]
    twins = []
    for level in range(4):
        for c, span in enumerate(SPANS):
            order = ((c + 2) % 3, (c + 1) % 3, c)
            for made in waiting[c]:
                made.wait_recv()
            if level < 3:
                spot = {n: chip[n] for n in order[level:]}
                block = everyone.at[block_of((0, 1, 2), spot, (rep, every, span))]
                waiting[c] = []
                for k in range(1, SIDE):
                    waiting[c].append(copy(
                        block, block, up_send.at[level, c, k - 1], up_recv.at[level, c, k - 1],
                        moved(chip, order[level], k), rep,
                    ))
                    waiting[c][-1].start()
                sent += waiting[c]
            if level >= 2:
                for k in range(1 if level == 3 else 0, SIDE if level == 3 else 1):
                    spot = {c: lax.rem(chip[c] + SIDE - k, SIDE)}
                    block = everyone.at[block_of((0, 1, 2), spot, (rep, every, span))]
                    twins.append(copy(
                        block, block, twin_send.at[c, k], twin_recv.at[c, k], chip, other
                    ))
                    twins[-1].start()
    for made in twins:
        made.wait()
    for made in sent:
        made.wait_send()


def train_kernel(
    scale, x, wl, wt_t, at_t, lab, ml, vl, mt, vt, logits_out, everyone, gradient_out,
    wtb, hidden, slope, dpre, left, grads, *scratch,
):
    chip, rep = place()
    barrier = pltpu.get_barrier_semaphore()
    for axis in range(3):
        for k in range(1, SIDE):
            to = at(moved(chip, axis, k))
            pl.semaphore_signal(barrier, inc=1, device_id=(to, rep), device_id_type=MESH)
    pl.semaphore_signal(
        barrier, inc=1, device_id=(lax.axis_index("store"), 1 - rep), device_id_type=MESH
    )
    step_part(scale, x, wl, wt_t, at_t, lab, logits_out, grads, wtb, hidden, slope, dpre, left)
    pl.semaphore_wait(barrier, 10)
    reduce_part(chip, rep, grads, ml, vl, mt, vt, everyone, gradient_out, *scratch)


def train(x, weights_low, top_t, adjacency_t, labels, scale, ml, vl, mt, vt):
    near = x.shape[0]
    seeds = adjacency_t.shape[1]
    width = weights_low.shape[1]
    cube = (SIDE, SIDE, SIDE)
    tile = (16, width)
    vmem = pl.BlockSpec(memory_space=pltpu.VMEM)
    hops = pltpu.SemaphoreType.DMA((3, 3, 3))
    return pl.pallas_call(
        functools.partial(train_kernel, scale),
        out_shape=(
            jax.ShapeDtypeStruct((top_t.shape[0], seeds), F32),
            jax.ShapeDtypeStruct(cube + (2,) + tile, BF16),
            jax.ShapeDtypeStruct(tile, F32),
        ),
        in_specs=[vmem] * 9,
        out_specs=(vmem,) * 3,
        scratch_shapes=[
            pltpu.VMEM((256, 2 * width), BF16),
            pltpu.VMEM((near, width), BF16),
            pltpu.VMEM((near, width), F32),
            pltpu.VMEM((near, width), BF16),
            pltpu.VMEM((2 * width, near), BF16),
            pltpu.VMEM(cube + (2,) + tile, BF16),
            pltpu.VMEM(cube + tile, BF16),
            pltpu.VMEM(cube + tile, BF16),
            pltpu.VMEM((SIDE - 1, SIDE, SIDE) + tile, BF16),
            pltpu.VMEM((SIDE, SIDE) + tile, BF16),
            pltpu.VMEM((SIDE - 1, SIDE) + tile, BF16),
            pltpu.VMEM((SIDE,) + tile, BF16),
            pltpu.VMEM((SIDE - 1,) + tile, BF16),
            pltpu.VMEM(tile, F32),
            pltpu.VMEM((16, 256), F32),
            pltpu.SemaphoreType.DMA((3,)),
            pltpu.SemaphoreType.DMA((3,)),
            hops, hops, hops, hops,
            pltpu.SemaphoreType.DMA((3, SIDE)),
            pltpu.SemaphoreType.DMA((3, SIDE)),
        ],
        compiler_params=pltpu.CompilerParams(
            collective_id=1, has_side_effects=True, vmem_limit_bytes=40 << 20
        ),
    )(x, weights_low, top_t, adjacency_t, labels, ml, vl, mt, vt)


def finish_kernel(
    steps, gradient, logits, wl, wt_t, ml, vl, mt, vt,
    logits_out, wl_out, wt_t_out, ml_out, vl_out, mt_out, vt_out, top,
):
    classes = wt_t.shape[0]
    wl_out[...] = wl[...] - dot(spread_low(), steps[...])
    for m in range(2):
        rows = slice(256 * m, 256 * m + 256)
        step = jnp.zeros((256, 256), F32)
        for b in range(4):
            step = step + dot(spread_top(b), steps[rows, 256 * b : 256 * b + 256])
        wt_t_out[:, rows] = wt_t[:, rows] - jnp.transpose(step)[0:classes]

    @pl.when(pl.program_id(0) == 0)
    def _():
        logits_out[...] = logits[...]
        _, ml_out[...], vl_out[...] = adam_parts(ml[...], vl[...], gradient[0:12, :])
        top_rows(gradient, top)
        _, mt_out[...], vt_out[...] = adam_parts(mt[...], vt[...], top[:, 0:classes])


def finish(steps, gradient, logits, weights_low, top_t, ml, vl, mt, vt):
    rows, width = weights_low.shape
    classes, tops = top_t.shape
    low = pl.BlockSpec((384, width), lambda i: (i, 0))
    top = pl.BlockSpec((classes, 512), lambda i: (0, i))
    same = [pl.BlockSpec(each.shape, lambda i: (0, 0)) for each in (ml, vl, mt, vt)]
    share = pl.BlockSpec(gradient.shape, lambda i: (0, 0))
    scores = pl.BlockSpec(logits.shape, lambda i: (0, 0))
    return pl.pallas_call(
        finish_kernel,
        grid=(4,),
        out_shape=tuple(
            jax.ShapeDtypeStruct(each.shape, F32)
            for each in (logits, weights_low, top_t, ml, vl, mt, vt)
        ),
        in_specs=[pl.BlockSpec((512, width), lambda i: (i, 0)), share, scores, low, top] + same,
        out_specs=[scores, low, top] + same,
        scratch_shapes=[pltpu.VMEM((16, 256), F32)],
        compiler_params=pltpu.CompilerParams(vmem_limit_bytes=32 << 20),
    )(steps, gradient, logits, weights_low, top_t, ml, vl, mt, vt)


def per_device(
    features,
    owners_near,
    slots_near,
    owners_far,
    slots_far,
    adjacency_low,
    adjacency_top,
    labels,
    weights_low,
    weights_top,
    first_low,
    second_low,
    first_top,
    second_top,
):
    x = fetch(
        owners_near.T, slots_near.T, owners_far.T, slots_far.T, adjacency_low.T, features
    )
    members = lax.axis_size(("store", "rep"))
    scale = 1.0 / (labels.shape[0] * members)
    top_t = weights_top.T
    moments = (first_low, second_low, first_top, second_top)
    logits, steps, gradient = train(
        x, weights_low, top_t, adjacency_top.T, labels[None, :], scale, *moments
    )
    logits, new_low, new_top, new_first_low, new_second_low, new_first_top, new_second_top = finish(
        steps.reshape(-1, steps.shape[-1]), gradient, logits, weights_low, top_t, *moments
    )
    return (
        logits.T, new_low, new_first_low, new_second_low, new_top.T, new_first_top, new_second_top
    )


def solution(mesh):
    both = P(("store", "rep"), None)
    return jax.shard_map(
        per_device,
        mesh=mesh,
        in_specs=(
            P("store", None), both, both, both, both, both, both, P(("store", "rep")),
            P(), P(), both, both, both, both,
        ),
        out_specs=(both, P(), both, both, P(), both, both),
        check_vma=False,
    )
```

```python
import functools

import jax
import jax.numpy as jnp
from jax import lax
from jax.experimental import pallas as pl
from jax.experimental.pallas import tpu as pltpu
from jax.sharding import PartitionSpec as P

beta_one = 0.9
beta_two = 0.999
bias_one = 1.0 - 0.9**10
bias_two = 1.0 - 0.999**10
learn_rate = 0.01
adam_eps = 1e-08

MESH = pl.DeviceIdType.MESH
F32 = jnp.float32
BF16 = jnp.bfloat16
SIDE = 4
STORES = SIDE**3
CAP_NEAR = 16
CAP_FAR = 96
CAP = CAP_NEAR + CAP_FAR


def iota(shape, dim):
    return lax.broadcasted_iota(jnp.int32, shape, dim)


def dot(a, b):
    return jnp.dot(a, b, preferred_element_type=F32)


def dot_nt(a, b):
    return lax.dot_general(a, b, (((1,), (1,)), ((), ())), preferred_element_type=F32)


def place():
    store = lax.axis_index("store")
    return (store // 16, lax.rem(store // 4, 4), lax.rem(store, 4)), lax.axis_index("rep")


def at(chip):
    return (chip[0] * SIDE + chip[1]) * SIDE + chip[2]


def moved(chip, axis, step):
    return [lax.rem(c + step, SIDE) if n == axis else c for n, c in enumerate(chip)]


def partner(shift, chip, sign):
    steps = (shift // 16, lax.rem(shift // 4, 4), lax.rem(shift, 4))
    return at([lax.rem(c + sign * step + SIDE, SIDE) for c, step in zip(chip, steps)])


def routes():
    load = [[0] * 3 for _ in range(3)]
    found = {}
    by_hops = {1: [], 2: [], 3: []}
    for shift in range(1, STORES):
        steps = (shift // 16, shift // 4 % 4, shift % 4)
        by_hops[sum(step != 0 for step in steps)].append((shift, steps))
    for hops in (3, 2, 1):
        for shift, steps in by_hops[hops]:
            options = [
                [axis for axis in order if steps[axis]]
                for order in ((0, 1, 2), (1, 2, 0), (2, 0, 1), (0, 2, 1), (2, 1, 0), (1, 0, 2))
            ]
            cost = lambda order: sum(
                load[h][axis] * min(steps[axis], SIDE - steps[axis]) * (3 - h)
                for h, axis in enumerate(order)
            )
            order = min(options, key=cost)
            for h, axis in enumerate(order):
                load[h][axis] += min(steps[axis], SIDE - steps[axis])
            found[shift] = [(axis, steps[axis]) for axis in order]
    return found, *([shift for shift, _ in by_hops[hops]] for hops in (3, 2, 1))


ROUTES, THREE, TWO, ONE = routes()
LEAVE = THREE + TWO + ONE + [0]
ARRIVE = [0] + ONE + [shift for both in zip(TWO, THREE) for shift in both]
SEGMENTS = (1, 2, 4, 4, 5)
GROUPS = 8


def load_all(stored, here, sem):
    loads = [
        pltpu.make_async_copy(src, dst, sem.at[n]) for n, (src, dst) in enumerate(zip(stored, here))
    ]
    for made in loads:
        made.start()
    return loads


def fetch_kernel(
    own_near, slot_near, own_far, slot_far, adj, spots, feat, out,
    table, cols, chosen, req_out, req_in, asked, counts, selves, send, relay_one, relay_two, recv,
    total, marks,
    ask_send, ask_recv, send_one, send_two, send_three, recv_one, recv_two, recv_three,
):
    chip, rep = place()
    barrier = pltpu.get_barrier_semaphore()

    @pl.loop(1, STORES)
    def _(shift):
        pl.semaphore_signal(
            barrier, inc=1, device_id=(partner(shift, chip, 1), rep), device_id_type=MESH
        )

    table[...] = jnp.zeros_like(table)
    upper = (iota((256, 256), 0) < iota((256, 256), 1)).astype(BF16)
    base = jnp.zeros((STORES, 1), F32)
    high = jnp.zeros((STORES, 128), F32)
    low = jnp.zeros((STORES, 128), F32)
    near_rows = own_near.shape[1]
    near_blocks = near_rows // 256
    spot = spots[:, 0:1]
    for b in range(near_blocks + own_far.shape[1] // 256):
        far = b >= near_blocks
        if b == near_blocks:
            base = jnp.zeros((STORES, 1), F32)
        first = 256 * (b - near_blocks if far else b)
        owner = (own_far if far else own_near)[:, first : first + 256]
        wanted = (slot_far if far else slot_near)[:, first : first + 256]
        jx = (chip[0] - (owner >> 4)) & 3
        jy = (chip[1] - ((owner >> 2) & 3)) & 3
        jz = (chip[2] - (owner & 3)) & 3
        shift = jx * 16 + jy * 4 + jz
        owned = (iota((STORES, 256), 0) == shift).astype(F32)
        owned_bf = owned.astype(BF16)
        before = dot(owned_bf, upper) + base
        base = base + jnp.sum(owned, axis=1, keepdims=True)
        position = jnp.sum(owned * before, axis=0, keepdims=True)
        if far:
            position = position + CAP_NEAR
        arrival = jnp.sum(owned * spot, axis=0, keepdims=True)
        for half in range(2):
            part = slice(128 * half, 128 * half + 128)
            table[2 * b + half : 2 * b + half + 1, 0:128] = arrival[:, part]
            table[2 * b + half : 2 * b + half + 1, 128:256] = position[:, part]
        placed = (iota((128, 256), 0) == position.astype(jnp.int32)).astype(F32)
        high = high + dot_nt(owned_bf, (placed * (wanted >> 6).astype(F32)).astype(BF16))
        low = low + dot_nt(owned_bf, (placed * (wanted & 63).astype(F32)).astype(BF16))
    requests = (high * 64.0 + low).astype(jnp.int32)
    for shift in range(STORES):
        req_out[shift] = requests[shift : shift + 1, :]
    req_in[0] = requests[0:1, :]

    pl.semaphore_wait(barrier, STORES - 1)

    def ask(shift):
        return pltpu.make_async_remote_copy(
            src_ref=req_out.at[shift], dst_ref=req_in.at[shift],
            send_sem=ask_send.at[shift], recv_sem=ask_recv.at[shift],
            device_id=(partner(shift, chip, -1), rep), device_id_type=MESH,
        )

    @pl.loop(1, STORES)
    def _(shift):
        ask(shift).start()

    table_t = jnp.transpose(table[...]).astype(BF16)
    fan = adj.shape[0]
    cols[...] = jnp.zeros_like(cols)
    for k in range(fan + 1):
        entry = adj[k : k + 1, :] if k < fan else iota((1, near_rows), 1)
        row_mark = (iota((128, near_rows), 0) == (entry >> 7)).astype(F32).astype(BF16)
        found = dot(table_t, row_mark)
        column = found[0:128] * float(CAP if k < fan else CAP_NEAR) + found[128:256]
        picked = iota((128, near_rows), 0) == (entry & 127)
        cols[k : k + 1, :] = jnp.sum(jnp.where(picked, column, 0.0), axis=0, keepdims=True)
    for c in range(near_rows // 128):
        block = slice(128 * c, 128 * c + 128)
        chosen[block, :] = jnp.transpose(cols[:, block])

    @pl.loop(1, STORES)
    def _(shift):
        ask(shift).wait()

    lists = jnp.concatenate(
        [req_in[shift].astype(F32) for shift in LEAVE] + [jnp.zeros((64, 128), F32)], axis=0
    )
    asked[...] = jnp.transpose(lists)[0:CAP, :]

    hops = {}

    def go(shift, hop):
        route = ROUTES[shift]
        if hop == 0:
            src = send.at[LEAVE.index(shift)]
        elif hop == 1:
            src = relay_one.at[LEAVE.index(shift)]
        else:
            src = relay_two.at[LEAVE.index(shift)]
        if hop == len(route) - 1:
            dst = recv.at[ARRIVE.index(shift)]
        elif hop == 0:
            dst = relay_one.at[LEAVE.index(shift)]
        else:
            dst = relay_two.at[LEAVE.index(shift)]
        hops[shift, hop] = pltpu.make_async_remote_copy(
            src_ref=src, dst_ref=dst,
            send_sem=(send_one, send_two, send_three)[hop].at[shift],
            recv_sem=(recv_one, recv_two, recv_three)[hop].at[shift],
            device_id=(at(moved(chip, *route[hop])), rep), device_id_type=MESH,
        )
        hops[shift, hop].start()

    nodes = feat.shape[0]

    def pick(g):
        for m in range(4):
            lane = iota((CAP, 128), 1) == g * 4 + m
            row = jnp.sum(jnp.where(lane, asked[...], 0.0), axis=1, keepdims=True)
            row = row.astype(jnp.int32)
            for c in range(nodes // 512):
                marks[CAP * m : CAP * m + CAP, 512 * c : 512 * c + 512] = (
                    (iota((CAP, 512), 1) + 512 * c == row).astype(F32).astype(BF16)
                )
        for h in range(3):
            span = slice(256 * h, 256 * h + 256)
            rows = dot(marks[...], feat[:, span]).astype(BF16)
            for m in range(4):
                send[g * 4 + m, :, span] = rows[CAP * m : CAP * m + CAP]

    begin = 0
    for size in SEGMENTS:
        pl.loop(begin, begin + size)(pick)
        for shift in LEAVE[4 * begin : 4 * (begin + size)]:
            if shift and (shift in THREE or shift in TWO):
                go(shift, 0)
        begin += size
        for shift in {11: THREE[:13], 16: THREE[13:]}.get(begin, []):
            hops[shift, 0].wait_recv()
            go(shift, 1)
    recv[0] = send[STORES - 1]
    for shift in ONE:
        go(shift, 0)

    width = counts.shape[2]

    @pl.loop(0, near_rows // 32)
    def _(r):
        rows = pl.ds(pl.multiple_of(r * 32, 32), 32)
        picked = chosen[rows, :]
        for c in range(GROUPS):
            lane = (iota((32, width), 1) + width * c).astype(F32)
            tally = jnp.zeros((32, width), F32)
            for k in range(fan):
                tally = tally + jnp.where(lane == picked[:, k : k + 1], 1.0, 0.0)
            counts[c, rows, :] = tally.astype(BF16)
            lane = (iota((32, 128), 1) + 128 * c).astype(F32)
            selves[c, rows, :] = jnp.where(lane == picked[:, fan : fan + 1], 1.0, 0.0).astype(BF16)

    for shift in TWO:
        hops[shift, 0].wait_recv()
        go(shift, 1)
    for shift in THREE:
        hops[shift, 1].wait_recv()
        go(shift, 2)

    features = recv.shape[2]
    many = STORES // GROUPS
    for c in range(GROUPS):
        for shift in ARRIVE[many * c : many * (c + 1)]:
            if shift:
                hops[shift, len(ROUTES[shift]) - 1].wait_recv()
        for h in range(3):
            span = slice(256 * h, 256 * h + 256)
            block = recv[many * c : many * (c + 1), :, span].reshape(width, 256)
            nears = recv[many * c : many * (c + 1), 0:CAP_NEAR, span].reshape(128, 256)
            sums = dot(counts[c], block)
            same = dot(selves[c], nears).astype(BF16)
            if c:
                sums = sums + total[:, span]
                same = same + out[:, span]
            out[:, span] = same
            if c < GROUPS - 1:
                total[:, span] = sums
            else:
                out[:, features + 256 * h : features + 256 * h + 256] = (
                    sums / float(fan)
                ).astype(BF16)
    for made in hops.values():
        made.wait_send()


def fetch(owners_near, slots_near, owners_far, slots_far, adjacency, features):
    near = adjacency.shape[1]
    width = features.shape[1]
    vmem = pl.BlockSpec(memory_space=pltpu.VMEM)
    spots = jnp.array([[ARRIVE.index(shift)] * 128 for shift in range(STORES)], F32)
    rows = (CAP, width)
    many = pltpu.SemaphoreType.DMA((STORES,))
    return pl.pallas_call(
        fetch_kernel,
        out_shape=jax.ShapeDtypeStruct((near, 2 * width), BF16),
        in_specs=[vmem] * 7,
        out_specs=vmem,
        scratch_shapes=[
            pltpu.VMEM((128, 256), F32),
            pltpu.VMEM((128, near), F32),
            pltpu.VMEM((near, 128), F32),
            pltpu.VMEM((STORES, 1, 128), jnp.int32),
            pltpu.VMEM((STORES, 1, 128), jnp.int32),
            pltpu.VMEM((CAP, 128), F32),
            pltpu.VMEM((GROUPS, near, STORES // GROUPS * CAP), BF16),
            pltpu.VMEM((GROUPS, near, 128), BF16),
            pltpu.VMEM((STORES,) + rows, BF16),
            pltpu.VMEM((len(THREE) + len(TWO),) + rows, BF16),
            pltpu.VMEM((len(THREE),) + rows, BF16),
            pltpu.VMEM((STORES,) + rows, BF16),
            pltpu.VMEM((near, width), F32),
            pltpu.VMEM((4 * CAP, features.shape[0]), BF16),
            many, many, many, many, many, many, many, many,
        ],
        compiler_params=pltpu.CompilerParams(
            collective_id=0, has_side_effects=True, vmem_limit_bytes=60 << 20
        ),
    )(owners_near, slots_near, owners_far, slots_far, adjacency, spots, features)


def spread_low():
    row, column = iota((192, 256), 0), iota((192, 256), 1)
    inner = column & 15
    return ((inner < 12) & (row == 12 * (column >> 4) + inner)).astype(F32).astype(BF16)


def spread_low_t():
    column, row = iota((512, 384), 1), iota((512, 384), 0)
    inner = row & 15
    return ((inner < 12) & (column == 12 * (row >> 4) + inner)).astype(F32).astype(BF16)


def spread_top(b):
    row, column = iota((256, 256), 0), iota((256, 256), 1)
    inner = column & 15
    return (
        ((inner >= 12) & (row == (column & -16) + 4 * (inner - 12) + b)).astype(F32).astype(BF16)
    )


def spread_top_t(b):
    column, row = iota((256, 256), 1), iota((256, 256), 0)
    inner = row & 15
    return (
        ((inner >= 12) & (column == (row & -16) + 4 * (inner - 12) + b)).astype(F32).astype(BF16)
    )


def gelu_parts(v):
    root = 0.7978845608028654
    square = v * v
    t = jnp.tanh(root * (v + 0.044715 * (v * square)))
    gate = 0.5 * (1.0 + t)
    slope = gate + 0.5 * v * (1.0 - t * t) * (root * (1.0 + 3.0 * 0.044715 * square))
    return v * gate, slope


def step_part(
    scale, x, strips, fetched, wt_t, at_t, lab, logits_out,
    grads, wtb, hidden, slope, dpre, left, tops,
):
    classes = wt_t.shape[0]
    width = hidden.shape[1]
    fan, seeds = at_t.shape
    near = x.shape[0]
    wtb[...] = jnp.zeros_like(wtb)
    wtb[0:classes, :] = wt_t[...].astype(BF16)
    for n in range(width // 256):
        span = slice(256 * n, 256 * n + 256)
        fetched[n].wait()
        value, rise = gelu_parts(dot(x[...], strips[n].astype(BF16)))
        hidden[:, span] = value.astype(BF16)
        slope[:, span] = rise
    picks_t = jnp.zeros((near, seeds), F32)
    for k in range(fan):
        picks_t = picks_t + (iota((near, seeds), 0) == at_t[k : k + 1, :]).astype(F32)
    picks = jnp.transpose(picks_t).astype(BF16)
    picks_t = picks_t.astype(BF16)
    mean = (dot(picks, hidden[...]) / float(fan)).astype(BF16)
    own = hidden[0:seeds, :]
    logits = dot_nt(wtb[:, 0:width], own) + dot_nt(wtb[:, width : 2 * width], mean)
    logits_out[...] = logits[0:classes]
    line = iota(logits.shape, 0)
    powers = jnp.where(line < classes, jnp.exp(logits), 0.0)
    chances = powers / jnp.sum(powers, axis=0, keepdims=True)
    targets = (line == lab[...]).astype(F32)
    dlogits = jnp.transpose((chances - targets) * scale).astype(BF16)
    first = dot(dlogits, wtb[:, 0:width])
    second = dot(dlogits, wtb[:, width : 2 * width]) / float(fan)
    second_high = second.astype(BF16)
    second_low = (second - second_high.astype(F32)).astype(BF16)
    for n in range(width // 256):
        span = slice(256 * n, 256 * n + 256)
        back = dot(picks_t, second_high[:, span]) + dot(picks_t, second_low[:, span])
        dpre[seeds:near, span] = (back[seeds:near] * slope[seeds:near, span]).astype(BF16)
        dpre[0:seeds, span] = ((back[0:seeds] + first[:, span]) * slope[0:seeds, span]).astype(BF16)
    low_t = spread_low_t()
    for m in range(x.shape[1] // 384):
        left[512 * m : 512 * m + 512, :] = dot_nt(low_t, x[:, 384 * m : 384 * m + 384]).astype(BF16)
    for b in range(width // 256):
        top_t = spread_top_t(b)
        for m in range(2 * width // 256):
            source = own if m < width // 256 else mean
            at_col = 256 * (m % (width // 256))
            tops[b, 256 * m : 256 * m + 256, :] = dot_nt(
                top_t, source[:, at_col : at_col + 256]
            ).astype(BF16)

    def gradient_span(span):
        for m in range(2 * width // 256):
            rows = slice(256 * m, 256 * m + 256)
            block = dot(left[rows, :], dpre[:, span])
            pieces = []
            lane = span.start
            while lane < span.stop:
                b = lane // 256
                stop = min(span.stop, 256 * b + 256)
                pieces.append(dot(tops[b, rows, :], dlogits[:, lane - 256 * b : stop - 256 * b]))
                lane = stop
            block = block + (pieces[0] if len(pieces) == 1 else jnp.concatenate(pieces, axis=1))
            grads[m // 2, 2 * (m % 2) : 2 * (m % 2) + 2, :, :, :, span] = block.astype(BF16).reshape(
                2, SIDE, 2, 16, span.stop - span.start
            )

    return gradient_span


def adam_parts(moment, square, gradient):
    moment_new = beta_one * moment + (1.0 - beta_one) * gradient
    square_new = beta_two * square + (1.0 - beta_two) * gradient * gradient
    update = moment_new / bias_one / (jnp.sqrt(square_new / bias_two) + adam_eps)
    return learn_rate * update, moment_new, square_new


SPANS = (slice(0, 384), slice(384, 768), slice(768, 1024))


def top_rows(share, top):
    for a in range(4):
        for b in range(4):
            top[4 * a + b : 4 * a + b + 1, :] = share[12 + a : 13 + a, 256 * b : 256 * b + 256]


def block_of(axes, fixed, tail):
    return tuple(fixed.get(axis, slice(None)) for axis in axes) + tail


def reduce_part(
    gradient_span, chip, rep, grads, ml, vl, mt, vt, everyone, gradient_out,
    pair, halves, got_one, sum_one, got_two, sum_two, got_three, share, top,
    pair_send, pair_recv, down_send, down_recv, up_send, up_recv, twin_send, twin_recv,
):
    other = 1 - rep
    classes = mt.shape[1]
    every = slice(None)

    def copy(src, dst, send_sem, recv_sem, to, core):
        return pltpu.make_async_remote_copy(
            src_ref=src, dst_ref=dst, send_sem=send_sem, recv_sem=recv_sem,
            device_id=(at(to), core), device_id_type=MESH,
        )

    swaps = []

    def start_swap(c):
        gradient_span(SPANS[c])
        swaps.append(copy(
            grads.at[:, :, :, other, :, SPANS[c]], pair.at[:, :, :, :, SPANS[c]],
            pair_send.at[c], pair_recv.at[c], chip, other,
        ))
        swaps[c].start()

    sent = []
    waiting = []
    start_swap(0)
    for c, span in enumerate(SPANS):
        if c < 2:
            start_swap(c + 1)
        swaps[c].wait_recv()

        @pl.loop(0, SIDE)
        def _(x):
            for y in range(SIDE):
                for z in range(SIDE):
                    halves[x, y, z, :, span] = (
                        grads[x, y, z, rep, :, span].astype(F32) + pair[x, y, z, :, span].astype(F32)
                    ).astype(BF16)

        axes, first = (0, 1, 2), c
        copies = []
        for k in range(1, SIDE):
            to = moved(chip, first, k)
            copies.append(copy(
                halves.at[block_of(axes, {first: to[first]}, (every, span))],
                got_one.at[k - 1, :, :, :, span],
                down_send.at[0, c, k - 1], down_recv.at[0, c, k - 1], to, rep,
            ))
            copies[-1].start()
        sent += copies
        waiting.append(copies)
    following = []
    for c, span in enumerate(SPANS):
        first, second = c, (c + 1) % 3
        left = tuple(n for n in range(3) if n != first)
        for made in waiting[c]:
            made.wait_recv()
        for a in range(SIDE):
            for b in range(SIDE):
                spot = {left[0]: a, left[1]: b, first: chip[first]}
                total = halves[block_of((0, 1, 2), spot, (every, span))].astype(F32)
                for k in range(1, SIDE):
                    total = total + got_one[k - 1, a, b, :, span].astype(F32)
                sum_one[a, b, :, span] = total.astype(BF16)
        copies = []
        for k in range(1, SIDE):
            to = moved(chip, second, k)
            copies.append(copy(
                sum_one.at[block_of(left, {second: to[second]}, (every, span))],
                got_two.at[k - 1, :, :, span],
                down_send.at[1, c, k - 1], down_recv.at[1, c, k - 1], to, rep,
            ))
            copies[-1].start()
        sent += copies
        following.append(copies)
    waiting, following = following, []
    for c, span in enumerate(SPANS):
        first, second, third = c, (c + 1) % 3, (c + 2) % 3
        left = tuple(n for n in range(3) if n != first)
        for made in waiting[c]:
            made.wait_recv()
        for a in range(SIDE):
            spot = {third: a, second: chip[second]}
            total = sum_one[block_of(left, spot, (every, span))].astype(F32)
            for k in range(1, SIDE):
                total = total + got_two[k - 1, a, :, span].astype(F32)
            sum_two[a, :, span] = total.astype(BF16)
        copies = []
        for k in range(1, SIDE):
            to = moved(chip, third, k)
            copies.append(copy(
                sum_two.at[to[third], :, span], got_three.at[k - 1, :, span],
                down_send.at[2, c, k - 1], down_recv.at[2, c, k - 1], to, rep,
            ))
            copies[-1].start()
        sent += copies
        following.append(copies)
    for c, span in enumerate(SPANS):
        for made in following[c]:
            made.wait_recv()
        total = sum_two[chip[(c + 2) % 3], :, span].astype(F32)
        for k in range(1, SIDE):
            total = total + got_three[k - 1, :, span].astype(F32)
        share[:, span] = total

    gradient_out[...] = share[...]
    top_rows(share, top)
    share[0:12, :] = adam_parts(ml[...], vl[...], share[0:12, :])[0]
    step = adam_parts(mt[...], vt[...], top[:, 0:classes])[0]
    top[:, 0:classes] = step
    for a in range(4):
        for b in range(4):
            share[12 + a : 13 + a, 256 * b : 256 * b + 256] = top[4 * a + b : 4 * a + b + 1, :]
    everyone[chip[0], chip[1], chip[2], rep] = share[...].astype(BF16)

    waiting = [[] for span in SPANS]
    twins = []
    for level in range(4):
        for c, span in enumerate(SPANS):
            order = ((c + 2) % 3, (c + 1) % 3, c)
            for made in waiting[c]:
                made.wait_recv()
            if level < 3:
                spot = {n: chip[n] for n in order[level:]}
                block = everyone.at[block_of((0, 1, 2), spot, (rep, every, span))]
                waiting[c] = []
                for k in range(1, SIDE):
                    waiting[c].append(copy(
                        block, block, up_send.at[level, c, k - 1], up_recv.at[level, c, k - 1],
                        moved(chip, order[level], k), rep,
                    ))
                    waiting[c][-1].start()
                sent += waiting[c]
            if level >= 2:
                for k in range(1 if level == 3 else 0, SIDE if level == 3 else 1):
                    spot = {c: lax.rem(chip[c] + SIDE - k, SIDE)}
                    block = everyone.at[block_of((0, 1, 2), spot, (rep, every, span))]
                    twins.append(copy(
                        block, block, twin_send.at[c, k], twin_recv.at[c, k], chip, other
                    ))
                    twins[-1].start()
    for made in twins:
        made.wait()
    for made in sent + swaps:
        made.wait_send()


def train_kernel(
    scale, x, wl, *refs,
):
    stored, (logits_out, everyone, gradient_out), refs = refs[:7], refs[7:10], refs[10:]
    here, load_sem, strips, strip_sem, refs = refs[:7], refs[7], refs[8], refs[9], refs[10:]
    wt_t, at_t, lab, ml, vl, mt, vt = here
    wtb, hidden, slope, dpre, left, tops, grads, *scratch = refs
    strip = strips.shape[2]
    fetched = [
        pltpu.make_async_copy(
            wl.at[:, strip * n : strip * n + strip], strips.at[n], strip_sem.at[n]
        )
        for n in range(strips.shape[0])
    ]
    for made in fetched:
        made.start()
    loads = load_all(stored, here, load_sem)
    chip, rep = place()
    barrier = pltpu.get_barrier_semaphore()
    for axis in range(3):
        for k in range(1, SIDE):
            to = at(moved(chip, axis, k))
            pl.semaphore_signal(barrier, inc=1, device_id=(to, rep), device_id_type=MESH)
    pl.semaphore_signal(
        barrier, inc=1, device_id=(lax.axis_index("store"), 1 - rep), device_id_type=MESH
    )
    for made in loads:
        made.wait()
    gradient_span = step_part(
        scale, x, strips, fetched, wt_t, at_t, lab, logits_out, grads, wtb, hidden, slope, dpre, left, tops
    )
    pl.semaphore_wait(barrier, 10)
    reduce_part(gradient_span, chip, rep, grads, ml, vl, mt, vt, everyone, gradient_out, *scratch)


def train(x, weights_low, top_t, adjacency_t, labels, scale, ml, vl, mt, vt):
    near = x.shape[0]
    seeds = adjacency_t.shape[1]
    width = weights_low.shape[1]
    given = (top_t, adjacency_t, labels, ml, vl, mt, vt)
    hbm = pl.BlockSpec(memory_space=pltpu.MemorySpace.HBM)
    cube = (SIDE, SIDE, SIDE)
    tile = (16, width)
    vmem = pl.BlockSpec(memory_space=pltpu.VMEM)
    hops = pltpu.SemaphoreType.DMA((3, 3, 3))
    return pl.pallas_call(
        functools.partial(train_kernel, scale),
        out_shape=(
            jax.ShapeDtypeStruct((top_t.shape[0], seeds), F32),
            jax.ShapeDtypeStruct(cube + (2,) + tile, BF16),
            jax.ShapeDtypeStruct(tile, F32),
        ),
        in_specs=[vmem] + [hbm] * 8,
        out_specs=(vmem,) * 3,
        scratch_shapes=[pltpu.VMEM(each.shape, each.dtype) for each in given]
        + [
            pltpu.SemaphoreType.DMA((len(given),)),
            pltpu.VMEM((width // 256, weights_low.shape[0], 256), F32),
            pltpu.SemaphoreType.DMA((width // 256,)),
            pltpu.VMEM((256, 2 * width), BF16),
            pltpu.VMEM((near, width), BF16),
            pltpu.VMEM((near, width), F32),
            pltpu.VMEM((near, width), BF16),
            pltpu.VMEM((2 * width, near), BF16),
            pltpu.VMEM((width // 256, 2 * width, seeds), BF16),
            pltpu.VMEM(cube + (2,) + tile, BF16),
            pltpu.VMEM(cube + tile, BF16),
            pltpu.VMEM(cube + tile, BF16),
            pltpu.VMEM((SIDE - 1, SIDE, SIDE) + tile, BF16),
            pltpu.VMEM((SIDE, SIDE) + tile, BF16),
            pltpu.VMEM((SIDE - 1, SIDE) + tile, BF16),
            pltpu.VMEM((SIDE,) + tile, BF16),
            pltpu.VMEM((SIDE - 1,) + tile, BF16),
            pltpu.VMEM(tile, F32),
            pltpu.VMEM((16, 256), F32),
            pltpu.SemaphoreType.DMA((3,)),
            pltpu.SemaphoreType.DMA((3,)),
            hops, hops, hops, hops,
            pltpu.SemaphoreType.DMA((3, SIDE)),
            pltpu.SemaphoreType.DMA((3, SIDE)),
        ],
        compiler_params=pltpu.CompilerParams(
            collective_id=1, has_side_effects=True, vmem_limit_bytes=44 << 20
        ),
    )(x, weights_low, *given)


def finish_kernel(
    steps, gradient, logits, wl, wt_t, ml, vl, mt, vt,
    logits_out, wl_out, wt_t_out, ml_out, vl_out, mt_out, vt_out, top,
):
    classes = wt_t.shape[0]
    wl_out[...] = wl[...] - dot(spread_low(), steps[...])
    step = jnp.zeros((256, 256), F32)
    for b in range(4):
        step = step + dot(spread_top(b), steps[:, 256 * b : 256 * b + 256])
    wt_t_out[...] = wt_t[...] - jnp.transpose(step)[0:classes]

    @pl.when(pl.program_id(0) == 0)
    def _():
        logits_out[...] = logits[...]
        _, ml_out[...], vl_out[...] = adam_parts(ml[...], vl[...], gradient[0:12, :])
        top_rows(gradient, top)
        _, mt_out[...], vt_out[...] = adam_parts(mt[...], vt[...], top[:, 0:classes])


def finish(steps, gradient, logits, weights_low, top_t, ml, vl, mt, vt):
    rows, width = weights_low.shape
    classes, tops = top_t.shape
    low = pl.BlockSpec((192, width), lambda i: (i, 0))
    top = pl.BlockSpec((classes, 256), lambda i: (0, i))
    same = [pl.BlockSpec(each.shape, lambda i: (0, 0)) for each in (ml, vl, mt, vt)]
    share = pl.BlockSpec(gradient.shape, lambda i: (0, 0))
    scores = pl.BlockSpec(logits.shape, lambda i: (0, 0))
    return pl.pallas_call(
        finish_kernel,
        grid=(8,),
        out_shape=tuple(
            jax.ShapeDtypeStruct(each.shape, F32)
            for each in (logits, weights_low, top_t, ml, vl, mt, vt)
        ),
        in_specs=[pl.BlockSpec((256, width), lambda i: (i, 0)), share, scores, low, top] + same,
        out_specs=[scores, low, top] + same,
        scratch_shapes=[pltpu.VMEM((16, 256), F32)],
        compiler_params=pltpu.CompilerParams(vmem_limit_bytes=32 << 20),
    )(steps, gradient, logits, weights_low, top_t, ml, vl, mt, vt)


def per_device(
    features,
    owners_near,
    slots_near,
    owners_far,
    slots_far,
    adjacency_low,
    adjacency_top,
    labels,
    weights_low,
    weights_top,
    first_low,
    second_low,
    first_top,
    second_top,
):
    x = fetch(
        owners_near.T, slots_near.T, owners_far.T, slots_far.T, adjacency_low.T, features
    )
    members = lax.axis_size(("store", "rep"))
    scale = 1.0 / (labels.shape[0] * members)
    top_t = weights_top.T
    moments = (first_low, second_low, first_top, second_top)
    logits, steps, gradient = train(
        x, weights_low, top_t, adjacency_top.T, labels[None, :], scale, *moments
    )
    logits, new_low, new_top, new_first_low, new_second_low, new_first_top, new_second_top = finish(
        steps.reshape(-1, steps.shape[-1]), gradient, logits, weights_low, top_t, *moments
    )
    return (
        logits.T, new_low, new_first_low, new_second_low, new_top.T, new_first_top, new_second_top
    )


def solution(mesh):
    both = P(("store", "rep"), None)
    return jax.shard_map(
        per_device,
        mesh=mesh,
        in_specs=(
            P("store", None), both, both, both, both, both, both, P(("store", "rep")),
            P(), P(), both, both, both, both,
        ),
        out_specs=(both, P(), both, both, P(), both, both),
        check_vma=False,
    )
```

```python
import functools

import jax
import jax.numpy as jnp
from jax import lax
from jax.experimental import pallas as pl
from jax.experimental.pallas import tpu as pltpu
from jax.sharding import PartitionSpec as P

beta_one = 0.9
beta_two = 0.999
bias_one = 1.0 - 0.9**10
bias_two = 1.0 - 0.999**10
learn_rate = 0.01
adam_eps = 1e-08

MESH = pl.DeviceIdType.MESH
F32 = jnp.float32
BF16 = jnp.bfloat16
SIDE = 4
STORES = SIDE**3
CAP_NEAR = 16
CAP_FAR = 96
CAP = CAP_NEAR + CAP_FAR


def iota(shape, dim):
    return lax.broadcasted_iota(jnp.int32, shape, dim)


def dot(a, b):
    return jnp.dot(a, b, preferred_element_type=F32)


def dot_nt(a, b):
    return lax.dot_general(a, b, (((1,), (1,)), ((), ())), preferred_element_type=F32)


def place():
    store = lax.axis_index("store")
    return (store // 16, lax.rem(store // 4, 4), lax.rem(store, 4)), lax.axis_index("rep")


def at(chip):
    return (chip[0] * SIDE + chip[1]) * SIDE + chip[2]


def moved(chip, axis, step):
    return [lax.rem(c + step, SIDE) if n == axis else c for n, c in enumerate(chip)]


def each_shift(chip, sign, act):
    x, y, z = [
        [lax.rem(c + sign * step + SIDE, SIDE) * scale for step in range(SIDE)]
        for c, scale in zip(chip, (SIDE * SIDE, SIDE, 1))
    ]
    for shift in range(1, STORES):
        act(shift, x[shift // 16] + y[shift // 4 % 4] + z[shift % 4])


def routes():
    load = [[0] * 3 for _ in range(3)]
    found = {}
    by_hops = {1: [], 2: [], 3: []}
    for shift in range(1, STORES):
        steps = (shift // 16, shift // 4 % 4, shift % 4)
        by_hops[sum(step != 0 for step in steps)].append((shift, steps))
    for hops in (3, 2, 1):
        for shift, steps in by_hops[hops]:
            options = [
                [axis for axis in order if steps[axis]]
                for order in ((0, 1, 2), (1, 2, 0), (2, 0, 1), (0, 2, 1), (2, 1, 0), (1, 0, 2))
            ]
            cost = lambda order: sum(
                load[h][axis] * min(steps[axis], SIDE - steps[axis]) * (3 - h)
                for h, axis in enumerate(order)
            )
            order = min(options, key=cost)
            for h, axis in enumerate(order):
                load[h][axis] += min(steps[axis], SIDE - steps[axis])
            found[shift] = [(axis, steps[axis]) for axis in order]
    return found, *([shift for shift, _ in by_hops[hops]] for hops in (3, 2, 1))


ROUTES, THREE, TWO, ONE = routes()
LEAVE = THREE + TWO + ONE + [0]
ARRIVE = [0] + ONE + [shift for both in zip(TWO, THREE) for shift in both]
SEGMENTS = (1, 2, 4, 4, 5)
GROUPS = 8


def load_all(stored, here, sem):
    loads = [
        pltpu.make_async_copy(src, dst, sem.at[n]) for n, (src, dst) in enumerate(zip(stored, here))
    ]
    for made in loads:
        made.start()
    return loads


def fetch_kernel(
    own_near, slot_near, own_far, slot_far, adj, spots, feat, out,
    table, cols, chosen, req_out, req_in, asked, counts, selves, send, relay_one, relay_two, recv,
    total, marks,
    ask_send, ask_recv, send_one, send_two, send_three, recv_one, recv_two, recv_three,
):
    chip, rep = place()
    barrier = pltpu.get_barrier_semaphore()

    def greet(shift, store):
        pl.semaphore_signal(barrier, inc=1, device_id=(store, rep), device_id_type=MESH)

    each_shift(chip, 1, greet)

    table[...] = jnp.zeros_like(table)
    upper = (iota((256, 256), 0) < iota((256, 256), 1)).astype(BF16)
    base = jnp.zeros((STORES, 1), F32)
    high = jnp.zeros((STORES, 128), F32)
    low = jnp.zeros((STORES, 128), F32)
    near_rows = own_near.shape[1]
    near_blocks = near_rows // 256
    spot = spots[:, 0:1]
    for b in range(near_blocks + own_far.shape[1] // 256):
        far = b >= near_blocks
        if b == near_blocks:
            base = jnp.zeros((STORES, 1), F32)
        first = 256 * (b - near_blocks if far else b)
        owner = (own_far if far else own_near)[:, first : first + 256]
        wanted = (slot_far if far else slot_near)[:, first : first + 256]
        jx = (chip[0] - (owner >> 4)) & 3
        jy = (chip[1] - ((owner >> 2) & 3)) & 3
        jz = (chip[2] - (owner & 3)) & 3
        shift = jx * 16 + jy * 4 + jz
        owned = (iota((STORES, 256), 0) == shift).astype(F32)
        owned_bf = owned.astype(BF16)
        before = dot(owned_bf, upper) + base
        base = base + jnp.sum(owned, axis=1, keepdims=True)
        position = jnp.sum(owned * before, axis=0, keepdims=True)
        if far:
            position = position + CAP_NEAR
        arrival = jnp.sum(owned * spot, axis=0, keepdims=True)
        for half in range(2):
            part = slice(128 * half, 128 * half + 128)
            table[2 * b + half : 2 * b + half + 1, 0:128] = arrival[:, part]
            table[2 * b + half : 2 * b + half + 1, 128:256] = position[:, part]
        placed = (iota((128, 256), 0) == position.astype(jnp.int32)).astype(F32)
        high = high + dot_nt(owned_bf, (placed * (wanted >> 6).astype(F32)).astype(BF16))
        low = low + dot_nt(owned_bf, (placed * (wanted & 63).astype(F32)).astype(BF16))
    requests = (high * 64.0 + low).astype(jnp.int32)
    for shift in range(STORES):
        req_out[shift] = requests[shift : shift + 1, :]
    req_in[0] = requests[0:1, :]

    pl.semaphore_wait(barrier, STORES - 1)

    asks = []

    def ask(shift, store):
        asks.append(pltpu.make_async_remote_copy(
            src_ref=req_out.at[shift], dst_ref=req_in.at[shift],
            send_sem=ask_send.at[shift], recv_sem=ask_recv.at[shift],
            device_id=(store, rep), device_id_type=MESH,
        ))
        asks[-1].start()

    each_shift(chip, -1, ask)

    table_t = jnp.transpose(table[...]).astype(BF16)
    fan = adj.shape[0]
    cols[...] = jnp.zeros_like(cols)
    for k in range(fan + 1):
        entry = adj[k : k + 1, :] if k < fan else iota((1, near_rows), 1)
        row_mark = (iota((128, near_rows), 0) == (entry >> 7)).astype(F32).astype(BF16)
        found = dot(table_t, row_mark)
        column = found[0:128] * float(CAP if k < fan else CAP_NEAR) + found[128:256]
        picked = iota((128, near_rows), 0) == (entry & 127)
        cols[k : k + 1, :] = jnp.sum(jnp.where(picked, column, 0.0), axis=0, keepdims=True)
    for c in range(near_rows // 128):
        block = slice(128 * c, 128 * c + 128)
        chosen[block, :] = jnp.transpose(cols[:, block])

    for made in asks:
        made.wait_recv()
    lists = jnp.concatenate(
        [req_in[shift].astype(F32) for shift in LEAVE] + [jnp.zeros((64, 128), F32)], axis=0
    )
    asked[...] = jnp.transpose(lists)[0:CAP, :]

    hops = {}

    def go(shift, hop):
        route = ROUTES[shift]
        if hop == 0:
            src = send.at[LEAVE.index(shift)]
        elif hop == 1:
            src = relay_one.at[LEAVE.index(shift)]
        else:
            src = relay_two.at[LEAVE.index(shift)]
        if hop == len(route) - 1:
            dst = recv.at[ARRIVE.index(shift)]
        elif hop == 0:
            dst = relay_one.at[LEAVE.index(shift)]
        else:
            dst = relay_two.at[LEAVE.index(shift)]
        hops[shift, hop] = pltpu.make_async_remote_copy(
            src_ref=src, dst_ref=dst,
            send_sem=(send_one, send_two, send_three)[hop].at[LEAVE.index(shift)],
            recv_sem=(recv_one, recv_two, recv_three)[hop].at[shift],
            device_id=(at(moved(chip, *route[hop])), rep), device_id_type=MESH,
        )
        hops[shift, hop].start()

    nodes = feat.shape[0]

    def pick(g):
        for m in range(4):
            lane = iota((CAP, 128), 1) == g * 4 + m
            row = jnp.sum(jnp.where(lane, asked[...], 0.0), axis=1, keepdims=True)
            row = row.astype(jnp.int32)
            for c in range(nodes // 512):
                marks[CAP * m : CAP * m + CAP, 512 * c : 512 * c + 512] = (
                    (iota((CAP, 512), 1) + 512 * c == row).astype(F32).astype(BF16)
                )
        for h in range(3):
            span = slice(256 * h, 256 * h + 256)
            rows = dot(marks[...], feat[:, span]).astype(BF16)
            for m in range(4):
                send[g * 4 + m, :, span] = rows[CAP * m : CAP * m + CAP]

    begin = 0
    for size in SEGMENTS:
        pl.loop(begin, begin + size)(pick)
        for shift in LEAVE[4 * begin : 4 * (begin + size)]:
            if shift and (shift in THREE or shift in TWO):
                go(shift, 0)
        begin += size
        for shift in {11: THREE[:13], 16: THREE[13:]}.get(begin, []):
            hops[shift, 0].wait_recv()
            go(shift, 1)
    recv[0] = send[STORES - 1]
    for shift in ONE:
        go(shift, 0)

    width = counts.shape[2]

    @pl.loop(0, near_rows // 32)
    def _(r):
        rows = pl.ds(pl.multiple_of(r * 32, 32), 32)
        picked = chosen[rows, :]
        for c in range(GROUPS):
            lane = (iota((32, width), 1) + width * c).astype(F32)
            tally = jnp.zeros((32, width), F32)
            for k in range(fan):
                tally = tally + jnp.where(lane == picked[:, k : k + 1], 1.0, 0.0)
            counts[c, rows, :] = tally.astype(BF16)
            lane = (iota((32, 128), 1) + 128 * c).astype(F32)
            selves[c, rows, :] = jnp.where(lane == picked[:, fan : fan + 1], 1.0, 0.0).astype(BF16)

    for shift in TWO:
        hops[shift, 0].wait_recv()
        go(shift, 1)
    for shift in THREE:
        hops[shift, 1].wait_recv()
        go(shift, 2)

    features = recv.shape[2]
    many = STORES // GROUPS
    for c in range(GROUPS):
        for shift in ARRIVE[many * c : many * (c + 1)]:
            if shift:
                hops[shift, len(ROUTES[shift]) - 1].wait_recv()
        for h in range(3):
            span = slice(256 * h, 256 * h + 256)
            block = recv[many * c : many * (c + 1), :, span].reshape(width, 256)
            nears = recv[many * c : many * (c + 1), 0:CAP_NEAR, span].reshape(128, 256)
            sums = dot(counts[c], block)
            same = dot(selves[c], nears).astype(BF16)
            if c:
                sums = sums + total[:, span]
                same = same + out[:, span]
            out[:, span] = same
            if c < GROUPS - 1:
                total[:, span] = sums
            else:
                out[:, features + 256 * h : features + 256 * h + 256] = (
                    sums / float(fan)
                ).astype(BF16)

    def sent(src, sem, begin, end):
        @pl.loop(begin, end)
        def _(n):
            pltpu.make_async_remote_copy(
                src_ref=src.at[n], dst_ref=src.at[n], send_sem=sem.at[n], recv_sem=sem.at[n],
                device_id=(at(moved(chip, 0, 1)), rep), device_id_type=MESH,
            ).wait_send()

    sent(req_out, ask_send, 1, STORES)
    sent(send, send_one, 0, STORES - 1)
    sent(relay_one, send_two, 0, len(THREE) + len(TWO))
    sent(relay_two, send_three, 0, len(THREE))


def fetch(owners_near, slots_near, owners_far, slots_far, adjacency, features):
    near = adjacency.shape[1]
    width = features.shape[1]
    vmem = pl.BlockSpec(memory_space=pltpu.VMEM)
    spots = jnp.array([[ARRIVE.index(shift)] * 128 for shift in range(STORES)], F32)
    rows = (CAP, width)
    many = pltpu.SemaphoreType.DMA((STORES,))
    return pl.pallas_call(
        fetch_kernel,
        out_shape=jax.ShapeDtypeStruct((near, 2 * width), BF16),
        in_specs=[vmem] * 7,
        out_specs=vmem,
        scratch_shapes=[
            pltpu.VMEM((128, 256), F32),
            pltpu.VMEM((128, near), F32),
            pltpu.VMEM((near, 128), F32),
            pltpu.VMEM((STORES, 1, 128), jnp.int32),
            pltpu.VMEM((STORES, 1, 128), jnp.int32),
            pltpu.VMEM((CAP, 128), F32),
            pltpu.VMEM((GROUPS, near, STORES // GROUPS * CAP), BF16),
            pltpu.VMEM((GROUPS, near, 128), BF16),
            pltpu.VMEM((STORES,) + rows, BF16),
            pltpu.VMEM((len(THREE) + len(TWO),) + rows, BF16),
            pltpu.VMEM((len(THREE),) + rows, BF16),
            pltpu.VMEM((STORES,) + rows, BF16),
            pltpu.VMEM((near, width), F32),
            pltpu.VMEM((4 * CAP, features.shape[0]), BF16),
            many, many, many, many, many, many, many, many,
        ],
        compiler_params=pltpu.CompilerParams(
            collective_id=0, has_side_effects=True, vmem_limit_bytes=60 << 20
        ),
    )(owners_near, slots_near, owners_far, slots_far, adjacency, spots, features)


def spread_low():
    row, column = iota((192, 256), 0), iota((192, 256), 1)
    inner = column & 15
    return ((inner < 12) & (row == 12 * (column >> 4) + inner)).astype(F32).astype(BF16)


def spread_low_t():
    column, row = iota((512, 384), 1), iota((512, 384), 0)
    inner = row & 15
    return ((inner < 12) & (column == 12 * (row >> 4) + inner)).astype(F32).astype(BF16)


def spread_top(b):
    row, column = iota((256, 256), 0), iota((256, 256), 1)
    inner = column & 15
    return (
        ((inner >= 12) & (row == (column & -16) + 4 * (inner - 12) + b)).astype(F32).astype(BF16)
    )


def spread_top_t(b):
    column, row = iota((256, 256), 1), iota((256, 256), 0)
    inner = row & 15
    return (
        ((inner >= 12) & (column == (row & -16) + 4 * (inner - 12) + b)).astype(F32).astype(BF16)
    )


def gelu_parts(v):
    root = 0.7978845608028654
    square = v * v
    t = jnp.tanh(root * (v + 0.044715 * (v * square)))
    gate = 0.5 * (1.0 + t)
    slope = gate + 0.5 * v * (1.0 - t * t) * (root * (1.0 + 3.0 * 0.044715 * square))
    return v * gate, slope


def step_part(
    scale, x, strips, fetched, wt_t, at_t, lab, logits_out,
    grads, wtb, hidden, slope, dpre, left, tops,
):
    classes = wt_t.shape[0]
    width = hidden.shape[1]
    fan, seeds = at_t.shape
    near = x.shape[0]
    wtb[...] = jnp.zeros_like(wtb)
    wtb[0:classes, :] = wt_t[...].astype(BF16)
    low_t = spread_low_t()
    for m in range(x.shape[1] // 384):
        left[512 * m : 512 * m + 512, :] = dot_nt(low_t, x[:, 384 * m : 384 * m + 384]).astype(BF16)
    for n in range(width // 256):
        span = slice(256 * n, 256 * n + 256)
        fetched[n].wait()
        value, rise = gelu_parts(dot(x[...], strips[n].astype(BF16)))
        hidden[:, span] = value.astype(BF16)
        slope[:, span] = rise
    picks_t = jnp.zeros((near, seeds), F32)
    for k in range(fan):
        picks_t = picks_t + (iota((near, seeds), 0) == at_t[k : k + 1, :]).astype(F32)
    picks = jnp.transpose(picks_t).astype(BF16)
    picks_t = picks_t.astype(BF16)
    mean = (dot(picks, hidden[...]) / float(fan)).astype(BF16)
    own = hidden[0:seeds, :]
    logits = dot_nt(wtb[:, 0:width], own) + dot_nt(wtb[:, width : 2 * width], mean)
    logits_out[...] = logits[0:classes]
    line = iota(logits.shape, 0)
    powers = jnp.where(line < classes, jnp.exp(logits), 0.0)
    chances = powers / jnp.sum(powers, axis=0, keepdims=True)
    targets = (line == lab[...]).astype(F32)
    dlogits = jnp.transpose((chances - targets) * scale).astype(BF16)
    first = dot(dlogits, wtb[:, 0:width])
    second = dot(dlogits, wtb[:, width : 2 * width]) / float(fan)
    second_high = second.astype(BF16)
    second_low = (second - second_high.astype(F32)).astype(BF16)
    for n in range(width // 256):
        span = slice(256 * n, 256 * n + 256)
        back = dot(picks_t, second_high[:, span]) + dot(picks_t, second_low[:, span])
        dpre[seeds:near, span] = (back[seeds:near] * slope[seeds:near, span]).astype(BF16)
        dpre[0:seeds, span] = ((back[0:seeds] + first[:, span]) * slope[0:seeds, span]).astype(BF16)
    for b in range(width // 256):
        top_t = spread_top_t(b)
        for m in range(2 * width // 256):
            source = own if m < width // 256 else mean
            at_col = 256 * (m % (width // 256))
            tops[b, 256 * m : 256 * m + 256, :] = dot_nt(
                top_t, source[:, at_col : at_col + 256]
            ).astype(BF16)

    def gradient_span(span):
        for m in range(2 * width // 256):
            rows = slice(256 * m, 256 * m + 256)
            block = dot(left[rows, :], dpre[:, span])
            pieces = []
            lane = span.start
            while lane < span.stop:
                b = lane // 256
                stop = min(span.stop, 256 * b + 256)
                pieces.append(dot(tops[b, rows, :], dlogits[:, lane - 256 * b : stop - 256 * b]))
                lane = stop
            block = block + (pieces[0] if len(pieces) == 1 else jnp.concatenate(pieces, axis=1))
            grads[m // 2, 2 * (m % 2) : 2 * (m % 2) + 2, :, :, :, span] = block.astype(BF16).reshape(
                2, SIDE, 2, 16, span.stop - span.start
            )

    return gradient_span


def adam_parts(moment, square, gradient):
    moment_new = beta_one * moment + (1.0 - beta_one) * gradient
    square_new = beta_two * square + (1.0 - beta_two) * gradient * gradient
    update = moment_new / bias_one / (jnp.sqrt(square_new / bias_two) + adam_eps)
    return learn_rate * update, moment_new, square_new


SPANS = (slice(0, 384), slice(384, 768), slice(768, 1024))


def top_rows(share, top):
    for a in range(4):
        for b in range(4):
            top[4 * a + b : 4 * a + b + 1, :] = share[12 + a : 13 + a, 256 * b : 256 * b + 256]


def block_of(axes, fixed, tail):
    return tuple(fixed.get(axis, slice(None)) for axis in axes) + tail


def reduce_part(
    gradient_span, chip, rep, grads, ml, vl, mt, vt, everyone, gradient_out,
    pair, halves, got_one, sum_one, got_two, sum_two, got_three, share, top,
    pair_send, pair_recv, down_send, down_recv, up_send, up_recv, twin_send, twin_recv,
):
    other = 1 - rep
    classes = mt.shape[1]
    every = slice(None)

    def copy(src, dst, send_sem, recv_sem, to, core):
        return pltpu.make_async_remote_copy(
            src_ref=src, dst_ref=dst, send_sem=send_sem, recv_sem=recv_sem,
            device_id=(at(to), core), device_id_type=MESH,
        )

    swaps = []

    def start_swap(c):
        gradient_span(SPANS[c])
        swaps.append(copy(
            grads.at[:, :, :, other, :, SPANS[c]], pair.at[:, :, :, :, SPANS[c]],
            pair_send.at[c], pair_recv.at[c], chip, other,
        ))
        swaps[c].start()

    sent = []
    waiting = []
    start_swap(0)
    for c, span in enumerate(SPANS):
        if c < 2:
            start_swap(c + 1)
        swaps[c].wait_recv()

        @pl.loop(0, SIDE)
        def _(x):
            for y in range(SIDE):
                for z in range(SIDE):
                    halves[x, y, z, :, span] = (
                        grads[x, y, z, rep, :, span].astype(F32) + pair[x, y, z, :, span].astype(F32)
                    ).astype(BF16)

        axes, first = (0, 1, 2), c
        copies = []
        for k in range(1, SIDE):
            to = moved(chip, first, k)
            copies.append(copy(
                halves.at[block_of(axes, {first: to[first]}, (every, span))],
                got_one.at[k - 1, :, :, :, span],
                down_send.at[0, c, k - 1], down_recv.at[0, c, k - 1], to, rep,
            ))
            copies[-1].start()
        sent += copies
        waiting.append(copies)
    following = []
    for c, span in enumerate(SPANS):
        first, second = c, (c + 1) % 3
        left = tuple(n for n in range(3) if n != first)
        for made in waiting[c]:
            made.wait_recv()

        @pl.loop(0, SIDE)
        def _(a):
            for b in range(SIDE):
                spot = {left[0]: a, left[1]: b, first: chip[first]}
                total = halves[block_of((0, 1, 2), spot, (every, span))].astype(F32)
                for k in range(1, SIDE):
                    total = total + got_one[k - 1, a, b, :, span].astype(F32)
                sum_one[a, b, :, span] = total.astype(BF16)

        copies = []
        for k in range(1, SIDE):
            to = moved(chip, second, k)
            copies.append(copy(
                sum_one.at[block_of(left, {second: to[second]}, (every, span))],
                got_two.at[k - 1, :, :, span],
                down_send.at[1, c, k - 1], down_recv.at[1, c, k - 1], to, rep,
            ))
            copies[-1].start()
        sent += copies
        following.append(copies)
    waiting, following = following, []
    for c, span in enumerate(SPANS):
        first, second, third = c, (c + 1) % 3, (c + 2) % 3
        left = tuple(n for n in range(3) if n != first)
        for made in waiting[c]:
            made.wait_recv()
        for a in range(SIDE):
            spot = {third: a, second: chip[second]}
            total = sum_one[block_of(left, spot, (every, span))].astype(F32)
            for k in range(1, SIDE):
                total = total + got_two[k - 1, a, :, span].astype(F32)
            sum_two[a, :, span] = total.astype(BF16)
        copies = []
        for k in range(1, SIDE):
            to = moved(chip, third, k)
            copies.append(copy(
                sum_two.at[to[third], :, span], got_three.at[k - 1, :, span],
                down_send.at[2, c, k - 1], down_recv.at[2, c, k - 1], to, rep,
            ))
            copies[-1].start()
        sent += copies
        following.append(copies)
    for c, span in enumerate(SPANS):
        for made in following[c]:
            made.wait_recv()
        total = sum_two[chip[(c + 2) % 3], :, span].astype(F32)
        for k in range(1, SIDE):
            total = total + got_three[k - 1, :, span].astype(F32)
        share[:, span] = total

    gradient_out[...] = share[...]
    top_rows(share, top)
    share[0:12, :] = adam_parts(ml[...], vl[...], share[0:12, :])[0]
    step = adam_parts(mt[...], vt[...], top[:, 0:classes])[0]
    top[:, 0:classes] = step
    for a in range(4):
        for b in range(4):
            share[12 + a : 13 + a, 256 * b : 256 * b + 256] = top[4 * a + b : 4 * a + b + 1, :]
    everyone[chip[0], chip[1], chip[2], rep] = share[...].astype(BF16)

    waiting = [[] for span in SPANS]
    twins = []
    for level in range(4):
        for c, span in enumerate(SPANS):
            order = ((c + 2) % 3, (c + 1) % 3, c)
            for made in waiting[c]:
                made.wait_recv()
            if level < 3:
                spot = {n: chip[n] for n in order[level:]}
                block = everyone.at[block_of((0, 1, 2), spot, (rep, every, span))]
                waiting[c] = []
                for k in range(1, SIDE):
                    waiting[c].append(copy(
                        block, block, up_send.at[level, c, k - 1], up_recv.at[level, c, k - 1],
                        moved(chip, order[level], k), rep,
                    ))
                    waiting[c][-1].start()
                sent += waiting[c]
            if level >= 2:
                for k in range(1 if level == 3 else 0, SIDE if level == 3 else 1):
                    spot = {c: lax.rem(chip[c] + SIDE - k, SIDE)}
                    block = everyone.at[block_of((0, 1, 2), spot, (rep, every, span))]
                    twins.append(copy(
                        block, block, twin_send.at[c, k], twin_recv.at[c, k], chip, other
                    ))
                    twins[-1].start()
    for made in twins:
        made.wait()
    for made in sent + swaps:
        made.wait_send()


def train_kernel(
    scale, x, wl, *refs,
):
    stored, (logits_out, everyone, gradient_out), refs = refs[:7], refs[7:10], refs[10:]
    here, load_sem, strips, strip_sem, refs = refs[:7], refs[7], refs[8], refs[9], refs[10:]
    wt_t, at_t, lab, ml, vl, mt, vt = here
    wtb, hidden, slope, dpre, left, tops, grads, *scratch = refs
    strip = strips.shape[2]
    fetched = [
        pltpu.make_async_copy(
            wl.at[:, strip * n : strip * n + strip], strips.at[n], strip_sem.at[n]
        )
        for n in range(strips.shape[0])
    ]
    for made in fetched:
        made.start()
    loads = load_all(stored, here, load_sem)
    chip, rep = place()
    barrier = pltpu.get_barrier_semaphore()
    for axis in range(3):
        for k in range(1, SIDE):
            to = at(moved(chip, axis, k))
            pl.semaphore_signal(barrier, inc=1, device_id=(to, rep), device_id_type=MESH)
    pl.semaphore_signal(
        barrier, inc=1, device_id=(lax.axis_index("store"), 1 - rep), device_id_type=MESH
    )
    for made in loads:
        made.wait()
    gradient_span = step_part(
        scale, x, strips, fetched, wt_t, at_t, lab, logits_out, grads, wtb, hidden, slope, dpre, left, tops
    )
    pl.semaphore_wait(barrier, 10)
    reduce_part(gradient_span, chip, rep, grads, ml, vl, mt, vt, everyone, gradient_out, *scratch)


def train(x, weights_low, top_t, adjacency_t, labels, scale, ml, vl, mt, vt):
    near = x.shape[0]
    seeds = adjacency_t.shape[1]
    width = weights_low.shape[1]
    given = (top_t, adjacency_t, labels, ml, vl, mt, vt)
    hbm = pl.BlockSpec(memory_space=pltpu.MemorySpace.HBM)
    cube = (SIDE, SIDE, SIDE)
    tile = (16, width)
    vmem = pl.BlockSpec(memory_space=pltpu.VMEM)
    hops = pltpu.SemaphoreType.DMA((3, 3, 3))
    return pl.pallas_call(
        functools.partial(train_kernel, scale),
        out_shape=(
            jax.ShapeDtypeStruct((top_t.shape[0], seeds), F32),
            jax.ShapeDtypeStruct(cube + (2,) + tile, BF16),
            jax.ShapeDtypeStruct(tile, F32),
        ),
        in_specs=[vmem] + [hbm] * 8,
        out_specs=(vmem,) * 3,
        scratch_shapes=[pltpu.VMEM(each.shape, each.dtype) for each in given]
        + [
            pltpu.SemaphoreType.DMA((len(given),)),
            pltpu.VMEM((width // 256, weights_low.shape[0], 256), F32),
            pltpu.SemaphoreType.DMA((width // 256,)),
            pltpu.VMEM((256, 2 * width), BF16),
            pltpu.VMEM((near, width), BF16),
            pltpu.VMEM((near, width), F32),
            pltpu.VMEM((near, width), BF16),
            pltpu.VMEM((2 * width, near), BF16),
            pltpu.VMEM((width // 256, 2 * width, seeds), BF16),
            pltpu.VMEM(cube + (2,) + tile, BF16),
            pltpu.VMEM(cube + tile, BF16),
            pltpu.VMEM(cube + tile, BF16),
            pltpu.VMEM((SIDE - 1, SIDE, SIDE) + tile, BF16),
            pltpu.VMEM((SIDE, SIDE) + tile, BF16),
            pltpu.VMEM((SIDE - 1, SIDE) + tile, BF16),
            pltpu.VMEM((SIDE,) + tile, BF16),
            pltpu.VMEM((SIDE - 1,) + tile, BF16),
            pltpu.VMEM(tile, F32),
            pltpu.VMEM((16, 256), F32),
            pltpu.SemaphoreType.DMA((3,)),
            pltpu.SemaphoreType.DMA((3,)),
            hops, hops, hops, hops,
            pltpu.SemaphoreType.DMA((3, SIDE)),
            pltpu.SemaphoreType.DMA((3, SIDE)),
        ],
        compiler_params=pltpu.CompilerParams(
            collective_id=1, has_side_effects=True, vmem_limit_bytes=44 << 20
        ),
    )(x, weights_low, *given)


def finish_kernel(
    steps, gradient, logits, wl, wt_t, ml, vl, mt, vt,
    logits_out, wl_out, wt_t_out, ml_out, vl_out, mt_out, vt_out, top, low_rows, top_rows_of,
):
    classes = wt_t.shape[0]

    @pl.when(pl.program_id(0) == 0)
    def _():
        low_rows[...] = spread_low()
        for b in range(4):
            top_rows_of[b] = spread_top(b)

    wl_out[...] = wl[...] - dot(low_rows[...], steps[...])
    step = jnp.zeros((256, 256), F32)
    for b in range(4):
        step = step + dot(top_rows_of[b], steps[:, 256 * b : 256 * b + 256])
    wt_t_out[...] = wt_t[...] - jnp.transpose(step)[0:classes]

    @pl.when(pl.program_id(0) == 0)
    def _():
        logits_out[...] = logits[...]
        _, ml_out[...], vl_out[...] = adam_parts(ml[...], vl[...], gradient[0:12, :])
        top_rows(gradient, top)
        _, mt_out[...], vt_out[...] = adam_parts(mt[...], vt[...], top[:, 0:classes])


def finish(steps, gradient, logits, weights_low, top_t, ml, vl, mt, vt):
    rows, width = weights_low.shape
    classes, tops = top_t.shape
    low = pl.BlockSpec((192, width), lambda i: (i, 0))
    top = pl.BlockSpec((classes, 256), lambda i: (0, i))
    same = [pl.BlockSpec(each.shape, lambda i: (0, 0)) for each in (ml, vl, mt, vt)]
    share = pl.BlockSpec(gradient.shape, lambda i: (0, 0))
    scores = pl.BlockSpec(logits.shape, lambda i: (0, 0))
    return pl.pallas_call(
        finish_kernel,
        grid=(8,),
        out_shape=tuple(
            jax.ShapeDtypeStruct(each.shape, F32)
            for each in (logits, weights_low, top_t, ml, vl, mt, vt)
        ),
        in_specs=[pl.BlockSpec((256, width), lambda i: (i, 0)), share, scores, low, top] + same,
        out_specs=[scores, low, top] + same,
        scratch_shapes=[
            pltpu.VMEM((16, 256), F32),
            pltpu.VMEM((192, 256), BF16),
            pltpu.VMEM((4, 256, 256), BF16),
        ],
        compiler_params=pltpu.CompilerParams(vmem_limit_bytes=32 << 20),
    )(steps, gradient, logits, weights_low, top_t, ml, vl, mt, vt)


def per_device(
    features,
    owners_near,
    slots_near,
    owners_far,
    slots_far,
    adjacency_low,
    adjacency_top,
    labels,
    weights_low,
    weights_top,
    first_low,
    second_low,
    first_top,
    second_top,
):
    x = fetch(
        owners_near.T, slots_near.T, owners_far.T, slots_far.T, adjacency_low.T, features
    )
    members = lax.axis_size(("store", "rep"))
    scale = 1.0 / (labels.shape[0] * members)
    top_t = weights_top.T
    moments = (first_low, second_low, first_top, second_top)
    logits, steps, gradient = train(
        x, weights_low, top_t, adjacency_top.T, labels[None, :], scale, *moments
    )
    logits, new_low, new_top, new_first_low, new_second_low, new_first_top, new_second_top = finish(
        steps.reshape(-1, steps.shape[-1]), gradient, logits, weights_low, top_t, *moments
    )
    return (
        logits.T, new_low, new_first_low, new_second_low, new_top.T, new_first_top, new_second_top
    )


def solution(mesh):
    both = P(("store", "rep"), None)
    return jax.shard_map(
        per_device,
        mesh=mesh,
        in_specs=(
            P("store", None), both, both, both, both, both, both, P(("store", "rep")),
            P(), P(), both, both, both, both,
        ),
        out_specs=(both, P(), both, both, P(), both, both),
        check_vma=False,
    )
```

```python
import functools

import jax
import jax.numpy as jnp
from jax import lax
from jax.experimental import pallas as pl
from jax.experimental.pallas import tpu as pltpu
from jax.sharding import PartitionSpec as P

beta_one = 0.9
beta_two = 0.999
bias_one = 1.0 - 0.9**10
bias_two = 1.0 - 0.999**10
learn_rate = 0.01
adam_eps = 1e-08

MESH = pl.DeviceIdType.MESH
F32 = jnp.float32
BF16 = jnp.bfloat16
SIDE = 4
STORES = SIDE**3
CAP_NEAR = 16
CAP_FAR = 96
CAP = CAP_NEAR + CAP_FAR


def iota(shape, dim):
    return lax.broadcasted_iota(jnp.int32, shape, dim)


def dot(a, b):
    return jnp.dot(a, b, preferred_element_type=F32)


def dot_nt(a, b):
    return lax.dot_general(a, b, (((1,), (1,)), ((), ())), preferred_element_type=F32)


def place():
    store = lax.axis_index("store")
    return (store // 16, lax.rem(store // 4, 4), lax.rem(store, 4)), lax.axis_index("rep")


def at(chip):
    return (chip[0] * SIDE + chip[1]) * SIDE + chip[2]


def moved(chip, axis, step):
    return [lax.rem(c + step, SIDE) if n == axis else c for n, c in enumerate(chip)]


PLANE = SIDE * SIDE


def peers(chip, sign):
    x, y, z = [
        [lax.rem(c + sign * step + SIDE, SIDE) * scale for step in range(SIDE)]
        for c, scale in zip(chip, (PLANE, SIDE, 1))
    ]
    line = [x[step] + y[0] + z[0] for step in range(SIDE)]
    return line, [x[0] + y[step // SIDE] + z[step % SIDE] for step in range(PLANE)]


def routes():
    load = [[0] * 3 for _ in range(3)]
    found = {}
    by_hops = {1: [], 2: [], 3: []}
    for shift in range(1, STORES):
        steps = (shift // 16, shift // 4 % 4, shift % 4)
        by_hops[sum(step != 0 for step in steps)].append((shift, steps))
    for hops in (3, 2, 1):
        for shift, steps in by_hops[hops]:
            options = [
                [axis for axis in order if steps[axis]]
                for order in ((0, 1, 2), (1, 2, 0), (2, 0, 1), (0, 2, 1), (2, 1, 0), (1, 0, 2))
            ]
            cost = lambda order: sum(
                load[h][axis] * min(steps[axis], SIDE - steps[axis]) * (3 - h)
                for h, axis in enumerate(order)
            )
            order = min(options, key=cost)
            for h, axis in enumerate(order):
                load[h][axis] += min(steps[axis], SIDE - steps[axis])
            found[shift] = [(axis, steps[axis]) for axis in order]
    return found, *([shift for shift, _ in by_hops[hops]] for hops in (3, 2, 1))


ROUTES, THREE, TWO, ONE = routes()
LEAVE = THREE + TWO + ONE + [0]
ARRIVE = [0] + ONE + [shift for both in zip(TWO, THREE) for shift in both]
SEGMENTS = (1, 2, 4, 4, 5)
GROUPS = 8


def load_all(stored, here, sem):
    loads = [
        pltpu.make_async_copy(src, dst, sem.at[n]) for n, (src, dst) in enumerate(zip(stored, here))
    ]
    for made in loads:
        made.start()
    return loads


def fetch_kernel(
    own_near, slot_near, own_far, slot_far, adj, spots, feat, out,
    table, cols, chosen, req_out, req_mid, req_in, asked, counts, selves, send, relay_one, relay_two, recv,
    total, marks,
    mid_send, mid_recv, ask_send, ask_recv, send_one, send_two, send_three, recv_one, recv_two, recv_three,
):
    chip, rep = place()
    barrier = pltpu.get_barrier_semaphore()

    line, plane = peers(chip, 1)
    for store in line[1:] + plane[1:]:
        pl.semaphore_signal(barrier, inc=1, device_id=(store, rep), device_id_type=MESH)

    table[...] = jnp.zeros_like(table)
    upper = (iota((256, 256), 0) < iota((256, 256), 1)).astype(BF16)
    base = jnp.zeros((STORES, 1), F32)
    high = jnp.zeros((STORES, 128), F32)
    low = jnp.zeros((STORES, 128), F32)
    near_rows = own_near.shape[1]
    near_blocks = near_rows // 256
    spot = spots[:, 0:1]
    blocks = range(near_blocks + own_far.shape[1] // 256)
    marked = []
    for b in blocks:
        far = b >= near_blocks
        if b == near_blocks:
            base = jnp.zeros((STORES, 1), F32)
        first = 256 * (b - near_blocks if far else b)
        owner = (own_far if far else own_near)[:, first : first + 256]
        wanted = (slot_far if far else slot_near)[:, first : first + 256]
        jx = (chip[0] - (owner >> 4)) & 3
        jy = (chip[1] - ((owner >> 2) & 3)) & 3
        jz = (chip[2] - (owner & 3)) & 3
        shift = jx * 16 + jy * 4 + jz
        owned = (iota((STORES, 256), 0) == shift).astype(F32)
        owned_bf = owned.astype(BF16)
        before = dot(owned_bf, upper) + base
        base = base + jnp.sum(owned, axis=1, keepdims=True)
        marked.append((wanted, owned, owned_bf, before))
    positions = []
    for b, (wanted, owned, owned_bf, before) in zip(blocks, marked):
        far = b >= near_blocks
        position = jnp.sum(owned * before, axis=0, keepdims=True)
        if far:
            position = position + CAP_NEAR
        arrival = jnp.sum(owned * spot, axis=0, keepdims=True)
        for half in range(2):
            part = slice(128 * half, 128 * half + 128)
            table[2 * b + half : 2 * b + half + 1, 0:128] = arrival[:, part]
            table[2 * b + half : 2 * b + half + 1, 128:256] = position[:, part]
        positions.append(position)
    for (wanted, owned, owned_bf, before), position in zip(marked, positions):
        placed = (iota((128, 256), 0) == position.astype(jnp.int32)).astype(F32)
        high = high + dot_nt(owned_bf, (placed * (wanted >> 6).astype(F32)).astype(BF16))
        low = low + dot_nt(owned_bf, (placed * (wanted & 63).astype(F32)).astype(BF16))
    requests = (high * 64.0 + low).astype(jnp.int32)
    for shift in range(STORES):
        held = req_out if shift >= PLANE else req_mid
        held[shift // PLANE, shift % PLANE] = requests[shift : shift + 1, :]

    pl.semaphore_wait(barrier, SIDE - 1 + PLANE - 1)

    line, plane = peers(chip, -1)

    def ask(src, dst, send_sem, recv_sem, store):
        made = pltpu.make_async_remote_copy(
            src_ref=src, dst_ref=dst, send_sem=send_sem, recv_sem=recv_sem,
            device_id=(store, rep), device_id_type=MESH,
        )
        made.start()
        return made

    asks = [
        ask(req_out.at[step], req_mid.at[step], mid_send.at[step], mid_recv.at[step], line[step])
        for step in range(1, SIDE)
    ]

    table_t = jnp.transpose(table[...]).astype(BF16)
    fan = adj.shape[0]
    cols[...] = jnp.zeros_like(cols)
    for k in range(fan + 1):
        if k == fan // 2:
            for made in asks:
                made.wait_recv()
            asks += [
                ask(
                    req_mid.at[:, step], req_in.at[:, step],
                    ask_send.at[step], ask_recv.at[step], plane[step],
                )
                for step in range(1, PLANE)
            ]
            req_in[:, 0] = req_mid[:, 0]
        entry = adj[k : k + 1, :] if k < fan else iota((1, near_rows), 1)
        row_mark = (iota((128, near_rows), 0) == (entry >> 7)).astype(F32).astype(BF16)
        found = dot(table_t, row_mark)
        column = found[0:128] * float(CAP if k < fan else CAP_NEAR) + found[128:256]
        picked = iota((128, near_rows), 0) == (entry & 127)
        cols[k : k + 1, :] = jnp.sum(jnp.where(picked, column, 0.0), axis=0, keepdims=True)
    for c in range(near_rows // 128):
        block = slice(128 * c, 128 * c + 128)
        chosen[block, :] = jnp.transpose(cols[:, block])

    for made in asks[SIDE - 1 :]:
        made.wait_recv()
    lists = jnp.concatenate(
        [req_in[shift // PLANE, shift % PLANE].astype(F32) for shift in LEAVE] + [jnp.zeros((64, 128), F32)], axis=0
    )
    asked[...] = jnp.transpose(lists)[0:CAP, :]

    hops = {}

    def go(shift, hop):
        route = ROUTES[shift]
        if hop == 0:
            src = send.at[LEAVE.index(shift)]
        elif hop == 1:
            src = relay_one.at[LEAVE.index(shift)]
        else:
            src = relay_two.at[LEAVE.index(shift)]
        if hop == len(route) - 1:
            dst = recv.at[ARRIVE.index(shift)]
        elif hop == 0:
            dst = relay_one.at[LEAVE.index(shift)]
        else:
            dst = relay_two.at[LEAVE.index(shift)]
        hops[shift, hop] = pltpu.make_async_remote_copy(
            src_ref=src, dst_ref=dst,
            send_sem=(send_one, send_two, send_three)[hop].at[LEAVE.index(shift)],
            recv_sem=(recv_one, recv_two, recv_three)[hop].at[shift],
            device_id=(at(moved(chip, *route[hop])), rep), device_id_type=MESH,
        )
        hops[shift, hop].start()

    nodes = feat.shape[0]

    def pick(g):
        for m in range(4):
            lane = iota((CAP, 128), 1) == g * 4 + m
            row = jnp.sum(jnp.where(lane, asked[...], 0.0), axis=1, keepdims=True)
            row = row.astype(jnp.int32)
            for c in range(nodes // 512):
                marks[CAP * m : CAP * m + CAP, 512 * c : 512 * c + 512] = (
                    (iota((CAP, 512), 1) + 512 * c == row).astype(F32).astype(BF16)
                )
        for h in range(3):
            span = slice(256 * h, 256 * h + 256)
            rows = dot(marks[...], feat[:, span]).astype(BF16)
            for m in range(4):
                send[g * 4 + m, :, span] = rows[CAP * m : CAP * m + CAP]

    begin = 0
    for size in SEGMENTS:
        pl.loop(begin, begin + size)(pick)
        for shift in LEAVE[4 * begin : 4 * (begin + size)]:
            if shift and (shift in THREE or shift in TWO):
                go(shift, 0)
        begin += size
        for shift in {11: THREE[:13], 16: THREE[13:]}.get(begin, []):
            hops[shift, 0].wait_recv()
            go(shift, 1)
    recv[0] = send[STORES - 1]
    for shift in ONE:
        go(shift, 0)

    width = counts.shape[2]

    @pl.loop(0, near_rows // 32)
    def _(r):
        rows = pl.ds(pl.multiple_of(r * 32, 32), 32)
        picked = chosen[rows, :]
        for c in range(GROUPS):
            lane = (iota((32, width), 1) + width * c).astype(F32)
            tally = jnp.zeros((32, width), F32)
            for k in range(fan):
                tally = tally + jnp.where(lane == picked[:, k : k + 1], 1.0, 0.0)
            counts[c, rows, :] = tally.astype(BF16)
            lane = (iota((32, 128), 1) + 128 * c).astype(F32)
            selves[c, rows, :] = jnp.where(lane == picked[:, fan : fan + 1], 1.0, 0.0).astype(BF16)

    for shift in TWO:
        hops[shift, 0].wait_recv()
        go(shift, 1)
    for shift in THREE:
        hops[shift, 1].wait_recv()
        go(shift, 2)

    features = recv.shape[2]
    many = STORES // GROUPS
    for c in range(GROUPS):
        for shift in ARRIVE[many * c : many * (c + 1)]:
            if shift:
                hops[shift, len(ROUTES[shift]) - 1].wait_recv()
        for h in range(3):
            span = slice(256 * h, 256 * h + 256)
            block = recv[many * c : many * (c + 1), :, span].reshape(width, 256)
            nears = recv[many * c : many * (c + 1), 0:CAP_NEAR, span].reshape(128, 256)
            sums = dot(counts[c], block)
            same = dot(selves[c], nears).astype(BF16)
            if c:
                sums = sums + total[:, span]
                same = same + out[:, span]
            out[:, span] = same
            if c < GROUPS - 1:
                total[:, span] = sums
            else:
                out[:, features + 256 * h : features + 256 * h + 256] = (
                    sums / float(fan)
                ).astype(BF16)

    def sent(src, sem, begin, end):
        @pl.loop(begin, end)
        def _(n):
            pltpu.make_async_remote_copy(
                src_ref=src.at[n], dst_ref=src.at[n], send_sem=sem.at[n], recv_sem=sem.at[n],
                device_id=(at(moved(chip, 0, 1)), rep), device_id_type=MESH,
            ).wait_send()

    for made in asks:
        made.wait_send()
    sent(send, send_one, 0, STORES - 1)
    sent(relay_one, send_two, 0, len(THREE) + len(TWO))
    sent(relay_two, send_three, 0, len(THREE))


def fetch(owners_near, slots_near, owners_far, slots_far, adjacency, features):
    near = adjacency.shape[1]
    width = features.shape[1]
    vmem = pl.BlockSpec(memory_space=pltpu.VMEM)
    spots = jnp.array([[ARRIVE.index(shift)] * 128 for shift in range(STORES)], F32)
    rows = (CAP, width)
    many = pltpu.SemaphoreType.DMA((STORES,))
    return pl.pallas_call(
        fetch_kernel,
        out_shape=jax.ShapeDtypeStruct((near, 2 * width), BF16),
        in_specs=[vmem] * 7,
        out_specs=vmem,
        scratch_shapes=[
            pltpu.VMEM((128, 256), F32),
            pltpu.VMEM((128, near), F32),
            pltpu.VMEM((near, 128), F32),
            pltpu.VMEM((SIDE, PLANE, 1, 128), jnp.int32),
            pltpu.VMEM((SIDE, PLANE, 1, 128), jnp.int32),
            pltpu.VMEM((SIDE, PLANE, 1, 128), jnp.int32),
            pltpu.VMEM((CAP, 128), F32),
            pltpu.VMEM((GROUPS, near, STORES // GROUPS * CAP), BF16),
            pltpu.VMEM((GROUPS, near, 128), BF16),
            pltpu.VMEM((STORES,) + rows, BF16),
            pltpu.VMEM((len(THREE) + len(TWO),) + rows, BF16),
            pltpu.VMEM((len(THREE),) + rows, BF16),
            pltpu.VMEM((STORES,) + rows, BF16),
            pltpu.VMEM((near, width), F32),
            pltpu.VMEM((4 * CAP, features.shape[0]), BF16),
            pltpu.SemaphoreType.DMA((SIDE,)),
            pltpu.SemaphoreType.DMA((SIDE,)),
            pltpu.SemaphoreType.DMA((PLANE,)),
            pltpu.SemaphoreType.DMA((PLANE,)),
            many, many, many, many, many, many,
        ],
        compiler_params=pltpu.CompilerParams(
            collective_id=0, has_side_effects=True, vmem_limit_bytes=60 << 20
        ),
    )(owners_near, slots_near, owners_far, slots_far, adjacency, spots, features)


def spread_low():
    row, column = iota((384, 512), 0), iota((384, 512), 1)
    inner = column & 15
    return ((inner < 12) & (row == 12 * (column >> 4) + inner)).astype(F32).astype(BF16)


def spread_low_t():
    column, row = iota((512, 384), 1), iota((512, 384), 0)
    inner = row & 15
    return ((inner < 12) & (column == 12 * (row >> 4) + inner)).astype(F32).astype(BF16)


def spread_top(b):
    row, column = iota((256, 256), 0), iota((256, 256), 1)
    inner = column & 15
    return (
        ((inner >= 12) & (row == (column & -16) + 4 * (inner - 12) + b)).astype(F32).astype(BF16)
    )


def spread_top_t(b):
    column, row = iota((256, 256), 1), iota((256, 256), 0)
    inner = row & 15
    return (
        ((inner >= 12) & (column == (row & -16) + 4 * (inner - 12) + b)).astype(F32).astype(BF16)
    )


def gelu_parts(v):
    root = 0.7978845608028654
    square = v * v
    t = jnp.tanh(root * (v + 0.044715 * (v * square)))
    gate = 0.5 * (1.0 + t)
    slope = gate + 0.5 * v * (1.0 - t * t) * (root * (1.0 + 3.0 * 0.044715 * square))
    return v * gate, slope


def step_part(
    scale, x, strips, fetched, wt_t, at_t, lab, logits_out,
    grads, wtb, hidden, slope, dpre, left, tops,
):
    classes = wt_t.shape[0]
    width = hidden.shape[1]
    fan, seeds = at_t.shape
    near = x.shape[0]
    wtb[...] = jnp.zeros_like(wtb)
    wtb[0:classes, :] = wt_t[...].astype(BF16)
    low_t = spread_low_t()
    for m in range(x.shape[1] // 384):
        left[512 * m : 512 * m + 512, :] = dot_nt(low_t, x[:, 384 * m : 384 * m + 384]).astype(BF16)
    for n in range(width // 256):
        span = slice(256 * n, 256 * n + 256)
        fetched[n].wait()
        value, rise = gelu_parts(dot(x[...], strips[n].astype(BF16)))
        hidden[:, span] = value.astype(BF16)
        slope[:, span] = rise
    picks_t = jnp.zeros((near, seeds), F32)
    for k in range(fan):
        picks_t = picks_t + (iota((near, seeds), 0) == at_t[k : k + 1, :]).astype(F32)
    picks = jnp.transpose(picks_t).astype(BF16)
    picks_t = picks_t.astype(BF16)
    mean = (dot(picks, hidden[...]) / float(fan)).astype(BF16)
    own = hidden[0:seeds, :]
    logits = dot_nt(wtb[:, 0:width], own) + dot_nt(wtb[:, width : 2 * width], mean)
    logits_out[...] = logits[0:classes]
    line = iota(logits.shape, 0)
    powers = jnp.where(line < classes, jnp.exp(logits), 0.0)
    chances = powers / jnp.sum(powers, axis=0, keepdims=True)
    targets = (line == lab[...]).astype(F32)
    dlogits = jnp.transpose((chances - targets) * scale).astype(BF16)
    first = dot(dlogits, wtb[:, 0:width])
    second = dot(dlogits, wtb[:, width : 2 * width]) / float(fan)
    second_high = second.astype(BF16)
    second_low = (second - second_high.astype(F32)).astype(BF16)
    for n in range(width // 256):
        span = slice(256 * n, 256 * n + 256)
        back = dot(picks_t, second_high[:, span]) + dot(picks_t, second_low[:, span])
        dpre[seeds:near, span] = (back[seeds:near] * slope[seeds:near, span]).astype(BF16)
        dpre[0:seeds, span] = ((back[0:seeds] + first[:, span]) * slope[0:seeds, span]).astype(BF16)
    for b in range(width // 256):
        top_t = spread_top_t(b)
        for m in range(2 * width // 256):
            source = own if m < width // 256 else mean
            at_col = 256 * (m % (width // 256))
            tops[b, 256 * m : 256 * m + 256, :] = dot_nt(
                top_t, source[:, at_col : at_col + 256]
            ).astype(BF16)

    def gradient_span(span):
        for m in range(2 * width // 256):
            rows = slice(256 * m, 256 * m + 256)
            block = dot(left[rows, :], dpre[:, span])
            pieces = []
            lane = span.start
            while lane < span.stop:
                b = lane // 256
                stop = min(span.stop, 256 * b + 256)
                pieces.append(dot(tops[b, rows, :], dlogits[:, lane - 256 * b : stop - 256 * b]))
                lane = stop
            block = block + (pieces[0] if len(pieces) == 1 else jnp.concatenate(pieces, axis=1))
            grads[m // 2, 2 * (m % 2) : 2 * (m % 2) + 2, :, :, :, span] = block.astype(BF16).reshape(
                2, SIDE, 2, 16, span.stop - span.start
            )

    return gradient_span


def adam_parts(moment, square, gradient):
    moment_new = beta_one * moment + (1.0 - beta_one) * gradient
    square_new = beta_two * square + (1.0 - beta_two) * gradient * gradient
    update = moment_new / bias_one / (jnp.sqrt(square_new / bias_two) + adam_eps)
    return learn_rate * update, moment_new, square_new


SPANS = (slice(0, 384), slice(384, 768), slice(768, 1024))


def top_rows(share, top):
    for a in range(4):
        for b in range(4):
            top[4 * a + b : 4 * a + b + 1, :] = share[12 + a : 13 + a, 256 * b : 256 * b + 256]


def block_of(axes, fixed, tail):
    return tuple(fixed.get(axis, slice(None)) for axis in axes) + tail


def reduce_part(
    gradient_span, chip, rep, grads, ml, vl, mt, vt, everyone, gradient_out,
    pair, halves, got_one, sum_one, got_two, sum_two, got_three, share, top,
    pair_send, pair_recv, down_send, down_recv, up_send, up_recv, twin_send, twin_recv,
):
    other = 1 - rep
    classes = mt.shape[1]
    every = slice(None)

    def copy(src, dst, send_sem, recv_sem, to, core):
        return pltpu.make_async_remote_copy(
            src_ref=src, dst_ref=dst, send_sem=send_sem, recv_sem=recv_sem,
            device_id=(at(to), core), device_id_type=MESH,
        )

    swaps = []

    def start_swap(c):
        gradient_span(SPANS[c])
        swaps.append(copy(
            grads.at[:, :, :, other, :, SPANS[c]], pair.at[:, :, :, :, SPANS[c]],
            pair_send.at[c], pair_recv.at[c], chip, other,
        ))
        swaps[c].start()

    sent = []
    waiting = []
    start_swap(0)
    for c, span in enumerate(SPANS):
        if c < 2:
            start_swap(c + 1)
        swaps[c].wait_recv()

        @pl.loop(0, SIDE)
        def _(x):
            for y in range(SIDE):
                for z in range(SIDE):
                    halves[x, y, z, :, span] = (
                        grads[x, y, z, rep, :, span].astype(F32) + pair[x, y, z, :, span].astype(F32)
                    ).astype(BF16)

        axes, first = (0, 1, 2), c
        copies = []
        for k in range(1, SIDE):
            to = moved(chip, first, k)
            copies.append(copy(
                halves.at[block_of(axes, {first: to[first]}, (every, span))],
                got_one.at[k - 1, :, :, :, span],
                down_send.at[0, c, k - 1], down_recv.at[0, c, k - 1], to, rep,
            ))
            copies[-1].start()
        sent += copies
        waiting.append(copies)
    following = []
    for c, span in enumerate(SPANS):
        first, second = c, (c + 1) % 3
        left = tuple(n for n in range(3) if n != first)
        for made in waiting[c]:
            made.wait_recv()

        @pl.loop(0, SIDE)
        def _(a):
            for b in range(SIDE):
                spot = {left[0]: a, left[1]: b, first: chip[first]}
                total = halves[block_of((0, 1, 2), spot, (every, span))].astype(F32)
                for k in range(1, SIDE):
                    total = total + got_one[k - 1, a, b, :, span].astype(F32)
                sum_one[a, b, :, span] = total.astype(BF16)

        copies = []
        for k in range(1, SIDE):
            to = moved(chip, second, k)
            copies.append(copy(
                sum_one.at[block_of(left, {second: to[second]}, (every, span))],
                got_two.at[k - 1, :, :, span],
                down_send.at[1, c, k - 1], down_recv.at[1, c, k - 1], to, rep,
            ))
            copies[-1].start()
        sent += copies
        following.append(copies)
    waiting, following = following, []
    for c, span in enumerate(SPANS):
        first, second, third = c, (c + 1) % 3, (c + 2) % 3
        left = tuple(n for n in range(3) if n != first)
        for made in waiting[c]:
            made.wait_recv()
        for a in range(SIDE):
            spot = {third: a, second: chip[second]}
            total = sum_one[block_of(left, spot, (every, span))].astype(F32)
            for k in range(1, SIDE):
                total = total + got_two[k - 1, a, :, span].astype(F32)
            sum_two[a, :, span] = total.astype(BF16)
        copies = []
        for k in range(1, SIDE):
            to = moved(chip, third, k)
            copies.append(copy(
                sum_two.at[to[third], :, span], got_three.at[k - 1, :, span],
                down_send.at[2, c, k - 1], down_recv.at[2, c, k - 1], to, rep,
            ))
            copies[-1].start()
        sent += copies
        following.append(copies)
    for c, span in enumerate(SPANS):
        for made in following[c]:
            made.wait_recv()
        total = sum_two[chip[(c + 2) % 3], :, span].astype(F32)
        for k in range(1, SIDE):
            total = total + got_three[k - 1, :, span].astype(F32)
        share[:, span] = total

    gradient_out[...] = share[...]
    top_rows(share, top)
    share[0:12, :] = adam_parts(ml[...], vl[...], share[0:12, :])[0]
    step = adam_parts(mt[...], vt[...], top[:, 0:classes])[0]
    top[:, 0:classes] = step
    for a in range(4):
        for b in range(4):
            share[12 + a : 13 + a, 256 * b : 256 * b + 256] = top[4 * a + b : 4 * a + b + 1, :]
    everyone[chip[0], chip[1], chip[2], rep] = share[...].astype(BF16)

    waiting = [[] for span in SPANS]
    twins = []
    for level in range(4):
        for c, span in enumerate(SPANS):
            order = ((c + 2) % 3, (c + 1) % 3, c)
            for made in waiting[c]:
                made.wait_recv()
            if level < 3:
                spot = {n: chip[n] for n in order[level:]}
                block = everyone.at[block_of((0, 1, 2), spot, (rep, every, span))]
                waiting[c] = []
                for k in range(1, SIDE):
                    waiting[c].append(copy(
                        block, block, up_send.at[level, c, k - 1], up_recv.at[level, c, k - 1],
                        moved(chip, order[level], k), rep,
                    ))
                    waiting[c][-1].start()
                sent += waiting[c]
            if level >= 2:
                for k in range(1 if level == 3 else 0, SIDE if level == 3 else 1):
                    spot = {c: lax.rem(chip[c] + SIDE - k, SIDE)}
                    block = everyone.at[block_of((0, 1, 2), spot, (rep, every, span))]
                    twins.append(copy(
                        block, block, twin_send.at[c, k], twin_recv.at[c, k], chip, other
                    ))
                    twins[-1].start()
    for made in twins:
        made.wait()
    for made in sent + swaps:
        made.wait_send()


def train_kernel(
    scale, x, wl, *refs,
):
    stored, (logits_out, everyone, gradient_out), refs = refs[:7], refs[7:10], refs[10:]
    here, load_sem, strips, strip_sem, refs = refs[:7], refs[7], refs[8], refs[9], refs[10:]
    wt_t, at_t, lab, ml, vl, mt, vt = here
    wtb, hidden, slope, dpre, left, tops, grads, *scratch = refs
    strip = strips.shape[2]
    fetched = [
        pltpu.make_async_copy(
            wl.at[:, strip * n : strip * n + strip], strips.at[n], strip_sem.at[n]
        )
        for n in range(strips.shape[0])
    ]
    for made in fetched:
        made.start()
    loads = load_all(stored, here, load_sem)
    chip, rep = place()
    barrier = pltpu.get_barrier_semaphore()
    for axis in range(3):
        for k in range(1, SIDE):
            to = at(moved(chip, axis, k))
            pl.semaphore_signal(barrier, inc=1, device_id=(to, rep), device_id_type=MESH)
    pl.semaphore_signal(
        barrier, inc=1, device_id=(lax.axis_index("store"), 1 - rep), device_id_type=MESH
    )
    for made in loads:
        made.wait()
    gradient_span = step_part(
        scale, x, strips, fetched, wt_t, at_t, lab, logits_out, grads, wtb, hidden, slope, dpre, left, tops
    )
    pl.semaphore_wait(barrier, 10)
    reduce_part(gradient_span, chip, rep, grads, ml, vl, mt, vt, everyone, gradient_out, *scratch)


def train(x, weights_low, top_t, adjacency_t, labels, scale, ml, vl, mt, vt):
    near = x.shape[0]
    seeds = adjacency_t.shape[1]
    width = weights_low.shape[1]
    given = (top_t, adjacency_t, labels, ml, vl, mt, vt)
    hbm = pl.BlockSpec(memory_space=pltpu.MemorySpace.HBM)
    cube = (SIDE, SIDE, SIDE)
    tile = (16, width)
    vmem = pl.BlockSpec(memory_space=pltpu.VMEM)
    hops = pltpu.SemaphoreType.DMA((3, 3, 3))
    return pl.pallas_call(
        functools.partial(train_kernel, scale),
        out_shape=(
            jax.ShapeDtypeStruct((top_t.shape[0], seeds), F32),
            jax.ShapeDtypeStruct(cube + (2,) + tile, BF16),
            jax.ShapeDtypeStruct(tile, F32),
        ),
        in_specs=[vmem] + [hbm] * 8,
        out_specs=(vmem,) * 3,
        scratch_shapes=[pltpu.VMEM(each.shape, each.dtype) for each in given]
        + [
            pltpu.SemaphoreType.DMA((len(given),)),
            pltpu.VMEM((width // 256, weights_low.shape[0], 256), F32),
            pltpu.SemaphoreType.DMA((width // 256,)),
            pltpu.VMEM((256, 2 * width), BF16),
            pltpu.VMEM((near, width), BF16),
            pltpu.VMEM((near, width), F32),
            pltpu.VMEM((near, width), BF16),
            pltpu.VMEM((2 * width, near), BF16),
            pltpu.VMEM((width // 256, 2 * width, seeds), BF16),
            pltpu.VMEM(cube + (2,) + tile, BF16),
            pltpu.VMEM(cube + tile, BF16),
            pltpu.VMEM(cube + tile, BF16),
            pltpu.VMEM((SIDE - 1, SIDE, SIDE) + tile, BF16),
            pltpu.VMEM((SIDE, SIDE) + tile, BF16),
            pltpu.VMEM((SIDE - 1, SIDE) + tile, BF16),
            pltpu.VMEM((SIDE,) + tile, BF16),
            pltpu.VMEM((SIDE - 1,) + tile, BF16),
            pltpu.VMEM(tile, F32),
            pltpu.VMEM((16, 256), F32),
            pltpu.SemaphoreType.DMA((3,)),
            pltpu.SemaphoreType.DMA((3,)),
            hops, hops, hops, hops,
            pltpu.SemaphoreType.DMA((3, SIDE)),
            pltpu.SemaphoreType.DMA((3, SIDE)),
        ],
        compiler_params=pltpu.CompilerParams(
            collective_id=1, has_side_effects=True, vmem_limit_bytes=44 << 20
        ),
    )(x, weights_low, *given)


def finish_kernel(
    steps, gradient, logits, wl, wt_t, ml, vl, mt, vt,
    logits_out, wl_out, wt_t_out, ml_out, vl_out, mt_out, vt_out, top, low_rows, top_rows_of,
):
    classes = wt_t.shape[0]

    @pl.when(pl.program_id(0) == 0)
    def _():
        low_rows[...] = spread_low()
        for b in range(4):
            top_rows_of[b] = spread_top(b)

    wl_out[...] = wl[...] - dot(low_rows[...], steps[...])
    for m in range(2):
        rows = slice(256 * m, 256 * m + 256)
        step = jnp.zeros((256, 256), F32)
        for b in range(4):
            step = step + dot(top_rows_of[b], steps[rows, 256 * b : 256 * b + 256])
        wt_t_out[:, rows] = wt_t[:, rows] - jnp.transpose(step)[0:classes]

    @pl.when(pl.program_id(0) == 0)
    def _():
        logits_out[...] = logits[...]
        _, ml_out[...], vl_out[...] = adam_parts(ml[...], vl[...], gradient[0:12, :])
        top_rows(gradient, top)
        _, mt_out[...], vt_out[...] = adam_parts(mt[...], vt[...], top[:, 0:classes])


def finish(steps, gradient, logits, weights_low, top_t, ml, vl, mt, vt):
    rows, width = weights_low.shape
    classes, tops = top_t.shape
    low = pl.BlockSpec((384, width), lambda i: (i, 0))
    top = pl.BlockSpec((classes, 512), lambda i: (0, i))
    same = [pl.BlockSpec(each.shape, lambda i: (0, 0)) for each in (ml, vl, mt, vt)]
    share = pl.BlockSpec(gradient.shape, lambda i: (0, 0))
    scores = pl.BlockSpec(logits.shape, lambda i: (0, 0))
    return pl.pallas_call(
        finish_kernel,
        grid=(4,),
        out_shape=tuple(
            jax.ShapeDtypeStruct(each.shape, F32)
            for each in (logits, weights_low, top_t, ml, vl, mt, vt)
        ),
        in_specs=[pl.BlockSpec((512, width), lambda i: (i, 0)), share, scores, low, top] + same,
        out_specs=[scores, low, top] + same,
        scratch_shapes=[
            pltpu.VMEM((16, 256), F32),
            pltpu.VMEM((384, 512), BF16),
            pltpu.VMEM((4, 256, 256), BF16),
        ],
        compiler_params=pltpu.CompilerParams(vmem_limit_bytes=32 << 20),
    )(steps, gradient, logits, weights_low, top_t, ml, vl, mt, vt)


def per_device(
    features,
    owners_near,
    slots_near,
    owners_far,
    slots_far,
    adjacency_low,
    adjacency_top,
    labels,
    weights_low,
    weights_top,
    first_low,
    second_low,
    first_top,
    second_top,
):
    x = fetch(
        owners_near.T, slots_near.T, owners_far.T, slots_far.T, adjacency_low.T, features
    )
    members = lax.axis_size(("store", "rep"))
    scale = 1.0 / (labels.shape[0] * members)
    top_t = weights_top.T
    moments = (first_low, second_low, first_top, second_top)
    logits, steps, gradient = train(
        x, weights_low, top_t, adjacency_top.T, labels[None, :], scale, *moments
    )
    logits, new_low, new_top, new_first_low, new_second_low, new_first_top, new_second_top = finish(
        steps.reshape(-1, steps.shape[-1]), gradient, logits, weights_low, top_t, *moments
    )
    return (
        logits.T, new_low, new_first_low, new_second_low, new_top.T, new_first_top, new_second_top
    )


def solution(mesh):
    both = P(("store", "rep"), None)
    return jax.shard_map(
        per_device,
        mesh=mesh,
        in_specs=(
            P("store", None), both, both, both, both, both, both, P(("store", "rep")),
            P(), P(), both, both, both, both,
        ),
        out_specs=(both, P(), both, both, P(), both, both),
        check_vma=False,
    )
```
